32 devices in a mesh: rep: 8 (over y, x, core), fsdp: 4 (over z).
Axes of the slice: x: 2, y: 2, z: 4, core: 2. Of those that a mesh axis runs over, the one named last changes fastest.
Arguments:
- tokens: bfloat16 [128, 256, 384], P(('rep', 'fsdp')), may hold values from -6 to 6
- cotangent: bfloat16 [128, 256, 384], P(('rep', 'fsdp')), may hold values from -6 to 6
- cond_table: bfloat16 [1000, 384], replicated, may hold values from -6 to 6
- labels: int32 [128], P(('rep', 'fsdp')), may hold values from 0 to 999
- counts: int32 [32], P(('rep', 'fsdp')), may hold values from 1 to 4, as said below
- mod_weight: float32 [384, 2304], P('fsdp'), may hold values from -0.3125 to 0.3125
- qkv_weight: float32 [384, 1152], P('fsdp'), may hold values from -0.3125 to 0.3125
- out_weight: float32 [384, 384], P('fsdp'), may hold values from -3.5 to 3.5
- up_weight: float32 [384, 1536], P('fsdp'), may hold values from -0.3125 to 0.3125
- down_weight: float32 [1536, 384], P('fsdp'), may hold values from -0.625 to 0.625
- biases: float32 [5376], P('fsdp'), may hold values from -1.8 to 1.8
- mod_mean: float32 [384, 2304], P('fsdp'), may hold values from -32 to 32
- qkv_mean: float32 [384, 1152], P('fsdp'), may hold values from -32 to 32
- out_mean: float32 [384, 384], P('fsdp'), may hold values from -32 to 32
- up_mean: float32 [384, 1536], P('fsdp'), may hold values from -32 to 32
- down_mean: float32 [1536, 384], P('fsdp'), may hold values from -32 to 32
- bias_mean: float32 [5376], P('fsdp'), may hold values from -32 to 32
- mod_square: float32 [384, 2304], P('fsdp'), may hold values from 0 to 410
- qkv_square: float32 [384, 1152], P('fsdp'), may hold values from 0 to 410
- out_square: float32 [384, 384], P('fsdp'), may hold values from 0 to 410
- up_square: float32 [384, 1536], P('fsdp'), may hold values from 0 to 410
- down_square: float32 [1536, 384], P('fsdp'), may hold values from 0 to 410
- bias_square: float32 [5376], P('fsdp'), may hold values from 0 to 410
Outputs:
- block_out: bfloat16 [128, 256, 384], P(('rep', 'fsdp'))
- token_grad: bfloat16 [128, 256, 384], P(('rep', 'fsdp'))
- table_grad: float32 [1000, 384], P('fsdp')
- mod_grad: float32 [384, 2304], P('fsdp')
- qkv_grad: float32 [384, 1152], P('fsdp')
- out_grad: float32 [384, 384], P('fsdp')
- up_grad: float32 [384, 1536], P('fsdp')
- down_grad: float32 [1536, 384], P('fsdp')
- bias_grad: float32 [5376], P('fsdp')
- mod_next: float32 [384, 2304], P('fsdp')
- qkv_next: float32 [384, 1152], P('fsdp')
- out_next: float32 [384, 384], P('fsdp')
- up_next: float32 [384, 1536], P('fsdp')
- down_next: float32 [1536, 384], P('fsdp')
- bias_next: float32 [5376], P('fsdp')
- mean_mod: float32 [384, 2304], P('fsdp')
- mean_qkv: float32 [384, 1152], P('fsdp')
- mean_out: float32 [384, 384], P('fsdp')
- mean_up: float32 [384, 1536], P('fsdp')
- mean_down: float32 [1536, 384], P('fsdp')
- mean_bias: float32 [5376], P('fsdp')
- square_mod: float32 [384, 2304], P('fsdp')
- square_qkv: float32 [384, 1152], P('fsdp')
- square_out: float32 [384, 384], P('fsdp')
- square_up: float32 [384, 1536], P('fsdp')
- square_down: float32 [1536, 384], P('fsdp')
- square_bias: float32 [5376], P('fsdp')
The draws below stay inside these ranges and needn't reach their ends.
Inputs may be any that keep to these rules, and one draw needn't show every extreme that they name: `counts`: live latents of each device; some device holds exactly 4.
All inputs are finite; a program needn't handle non-finite values.
Results may differ from the reference program's by a relative error of at most 0.03.
Values may be sent and summed in bfloat16 or wider, within the bound.
No kernel may reach another device: no remote copies, remote signals or barrier semaphores. Data moves between devices by JAX's collectives and lax.ppermute only.
A program may use at most 192 MiB of HBM per device.

```python
import math
import jax
import jax.numpy as jnp
from jax import lax

HEADS = 6
HD = 64
L = 256
CLASSES = 1000
CAP = 4
STEP = 5
D = 384
SLOTS = 128
DEVICES = 32


def draw_counts(key, part):
    keys = jax.random.split(jax.random.fold_in(key, 17), 4)
    first = jax.random.randint(keys[0], (DEVICES,), 1, CAP + 1)
    second = jax.random.randint(keys[1], (DEVICES,), 1, CAP + 1)
    third = jax.random.randint(keys[2], (DEVICES,), 1, CAP + 1)
    least = jnp.minimum(jnp.minimum(first, second), third)
    chosen = jax.random.randint(keys[3], (), 0, DEVICES)
    return jnp.where(jnp.arange(DEVICES) == chosen, CAP, least).astype(jnp.int32)


def second_moment(key, extent, salt):
    top = float(CAP * DEVICES * L // 80 + 1)
    keys = jax.random.split(jax.random.fold_in(key, salt), 1)
    spread = jax.random.uniform(keys[0], extent, jnp.float32)
    return (top * jnp.exp(-4.0 * math.log(10.0) * spread)).astype(jnp.float32)


def draw_mod_square(key, part):
    return second_moment(key, (D, 6 * D), 101)


def draw_qkv_square(key, part):
    return second_moment(key, (D, 3 * D), 102)


def draw_out_square(key, part):
    return second_moment(key, (D, D), 103)


def draw_up_square(key, part):
    return second_moment(key, (D, 4 * D), 104)


def draw_down_square(key, part):
    return second_moment(key, (4 * D, D), 105)


def draw_bias_square(key, part):
    return second_moment(key, (14 * D,), 106)


def place_ends(values, rng, smallest, high):
    shape = values.shape
    spot = [jax.random.randint(jax.random.fold_in(rng, axis), (), 0, shape[axis]) for axis in range(len(shape))]
    values = values.at[tuple(spot)].set(smallest)
    longest = shape.index(max(shape))
    spot[longest] = (spot[longest] + 1) % shape[longest]
    return values.at[tuple(spot)].set(high)


def block_scale(own_key, shape, cuts, low, top_value):
    def one(dim, parts):
        draws = jax.random.uniform(jax.random.fold_in(jax.random.fold_in(own_key, 6), dim), (parts,), jnp.float32, low / len(cuts), top_value / len(cuts))
        return jnp.repeat(jnp.exp(draws), shape[dim] // parts).reshape((-1,) + (1,) * (len(shape) - dim - 1))

    factor_of = one(*cuts[0])
    for cut in cuts[1:]:
        factor_of = factor_of * one(*cut)
    return factor_of


def bell_draw(own_key, shape, scale, reach, pieces=(), kind=jnp.bfloat16):
    entries = jax.random.normal(own_key, shape, jnp.float32) * scale
    if len(pieces) > 0:
        entries = block_scale(own_key, shape, pieces, -0.22, 0.18) * entries
    return jnp.clip(entries, min=-reach, max=reach).astype(kind)


def setup_inputs(seed: int = 0) -> dict:
    splits = jax.random.split(jax.random.key(seed), 24)
    return {
        "tokens": bell_draw(splits[0], (SLOTS, L, D), 1.0, 6.0, ((0, 32),)),
        "cotangent": bell_draw(splits[1], (SLOTS, L, D), 1.0, 6.0, ((0, 32),)),
        "cond_table": bell_draw(splits[2], (CLASSES, D), 1.0, 6.0),
        "labels": place_ends(jax.random.randint(splits[3], (SLOTS,), 0, CLASSES), jax.random.fold_in(splits[3], 1), 0, CLASSES - 1).astype(jnp.int32),
        "counts": draw_counts(jax.random.fold_in(splits[23], 71), 0),
        "mod_weight": bell_draw(splits[5], (D, 6 * D), D ** -0.5, 0.3125, ((0, 4),), jnp.float32),
        "qkv_weight": bell_draw(splits[6], (D, 3 * D), D ** -0.5, 0.3125, ((0, 4),), jnp.float32),
        "out_weight": bell_draw(splits[7], (D, D), (max(D // 128, 2)) ** -0.5, 3.5, ((0, 4),), jnp.float32),
        "up_weight": bell_draw(splits[8], (D, 4 * D), D ** -0.5, 0.3125, ((0, 4),), jnp.float32),
        "down_weight": bell_draw(splits[9], (4 * D, D), (D // 4) ** -0.5, 0.625, ((0, 4),), jnp.float32),
        "biases": bell_draw(splits[10], (14 * D,), 0.3, 1.8, ((0, 4),), jnp.float32),
        "mod_mean": bell_draw(splits[11], (D, 6 * D), (0.05 * (CAP * DEVICES * L // 3) ** 0.5), 32.0, ((0, 4),), jnp.float32),
        "qkv_mean": bell_draw(splits[12], (D, 3 * D), (0.05 * (CAP * DEVICES * L // 3) ** 0.5), 32.0, ((0, 4),), jnp.float32),
        "out_mean": bell_draw(splits[13], (D, D), (0.05 * (CAP * DEVICES * L // 3) ** 0.5), 32.0, ((0, 4),), jnp.float32),
        "up_mean": bell_draw(splits[14], (D, 4 * D), (0.05 * (CAP * DEVICES * L // 3) ** 0.5), 32.0, ((0, 4),), jnp.float32),
        "down_mean": bell_draw(splits[15], (4 * D, D), (0.05 * (CAP * DEVICES * L // 3) ** 0.5), 32.0, ((0, 4),), jnp.float32),
        "bias_mean": bell_draw(splits[16], (14 * D,), (0.05 * (CAP * DEVICES * L // 3) ** 0.5), 32.0, ((0, 4),), jnp.float32),
        "mod_square": draw_mod_square(jax.random.fold_in(splits[23], 71), 0),
        "qkv_square": draw_qkv_square(jax.random.fold_in(splits[23], 71), 0),
        "out_square": draw_out_square(jax.random.fold_in(splits[23], 71), 0),
        "up_square": draw_up_square(jax.random.fold_in(splits[23], 71), 0),
        "down_square": draw_down_square(jax.random.fold_in(splits[23], 71), 0),
        "bias_square": draw_bias_square(jax.random.fold_in(splits[23], 71), 0),
    }


norm_eps = 1e-06
beta_one = 0.9
beta_two = 0.999
adam_eps = 1e-08
learn_rate = 0.01
weight_decay = 0.1
gelu_coef = 0.7978845608
cubic_coef = 0.044715

def batched(pattern, left_op, right_op):
    return jnp.einsum(pattern, left_op.astype(jnp.float32), right_op.astype(jnp.float32))

def layer_norm(values):
    centre = values - lax.optimization_barrier(jnp.mean(values, axis=-1, keepdims=True))
    inverse = lax.rsqrt(lax.optimization_barrier(jnp.mean(centre * centre, axis=-1, keepdims=True)) + norm_eps)
    return (centre * inverse, inverse)

def norm_back(normed, inverse, upstream):
    return inverse * (upstream - lax.optimization_barrier(jnp.mean(upstream, axis=-1, keepdims=True)) - normed * lax.optimization_barrier(jnp.mean(upstream * normed, axis=-1, keepdims=True)))

def gelu_value(preact):
    return 0.5 * preact * (1.0 + jnp.tanh(gelu_coef * (preact + cubic_coef * preact * preact * preact)))

def gelu_slope(preact):
    tanh_value = jnp.tanh(gelu_coef * (preact + cubic_coef * preact * preact * preact))
    return 0.5 * (1.0 + tanh_value) + 0.5 * preact * (1.0 - tanh_value * tanh_value) * gelu_coef * (1.0 + 3.0 * cubic_coef * preact * preact)

def split_bias(bias_all, features):
    return (bias_all[:6 * features], bias_all[6 * features:8 * features], bias_all[8 * features:9 * features], bias_all[9 * features:13 * features], bias_all[13 * features:])

def forward_one(tokens, cond_row, weights):
    mod_w, qkv_w, out_w, up_w, down_w, bias_all = weights
    length, features = tokens.shape
    mod_bias, qv_bias, out_bias, up_bias, down_bias = split_bias(bias_all.astype(jnp.float32), features)
    activation = jax.nn.silu(cond_row.astype(jnp.float32)).astype(jnp.bfloat16)
    modulation = jnp.dot(activation[None, :], mod_w, preferred_element_type=jnp.float32)[0] + mod_bias
    shift_one, scale_one, gate_one, shift_two, scale_two, gate_two = jnp.split(modulation, 6)
    inputs = tokens.astype(jnp.float32)
    normed_one, inv_one = layer_norm(inputs)
    h_one = (normed_one * (1.0 + scale_one) + shift_one).astype(jnp.bfloat16)
    qkv_bias = jnp.concatenate([qv_bias[:features], jnp.zeros((features,), jnp.float32), qv_bias[features:]])
    qkv_rows = (jnp.dot(h_one, qkv_w, preferred_element_type=jnp.float32) + qkv_bias).astype(jnp.bfloat16)
    queries = qkv_rows[:, :features].reshape(length, HEADS, HD)
    keys_h = qkv_rows[:, features:2 * features].reshape(length, HEADS, HD)
    values_h = qkv_rows[:, 2 * features:].reshape(length, HEADS, HD)
    scores = batched('qhd,khd->hqk', queries, keys_h) * HD ** (-0.5)
    exponent = jnp.exp(scores)
    row_total = lax.optimization_barrier(jnp.sum(exponent, axis=-1, keepdims=True))
    log_total = jnp.log(row_total[:, :, 0])
    probabilities = (exponent / row_total).astype(jnp.bfloat16)
    attn_out = batched('hqk,khd->qhd', probabilities, values_h).reshape(length, features).astype(jnp.bfloat16)
    attn_proj = jnp.dot(attn_out, out_w, preferred_element_type=jnp.float32) + out_bias
    residual = inputs + gate_one * attn_proj
    normed_two, inv_two = layer_norm(residual)
    h_two = (normed_two * (1.0 + scale_two) + shift_two).astype(jnp.bfloat16)
    preact = jnp.dot(h_two, up_w, preferred_element_type=jnp.float32) + up_bias
    hidden = gelu_value(preact).astype(jnp.bfloat16)
    mlp_out = jnp.dot(hidden, down_w, preferred_element_type=jnp.float32) + down_bias
    block_value = (residual + gate_two * mlp_out).astype(jnp.bfloat16)
    kept = (activation, modulation, normed_one, inv_one, h_one, qkv_rows, log_total, attn_out, attn_proj, normed_two, inv_two, h_two, preact, hidden, mlp_out)
    return (block_value, kept)

def backward_one(cotangent, cond_row, weights, kept):
    mod_w, qkv_w, out_w, up_w, down_w, bias_all = weights
    activation, modulation, normed_one, inv_one, h_one, qkv_rows, log_total, attn_out, attn_proj, normed_two, inv_two, h_two, preact, hidden, mlp_out = kept
    length, features = cotangent.shape
    shift_one, scale_one, gate_one, shift_two, scale_two, gate_two = jnp.split(modulation, 6)
    upstream = cotangent.astype(jnp.float32)
    d_gate_two = lax.optimization_barrier(jnp.sum(upstream * mlp_out, axis=0))
    e_mlp = upstream * gate_two
    d_mlp = e_mlp.astype(jnp.bfloat16)
    grad_down = jnp.dot(hidden.T, d_mlp, preferred_element_type=jnp.float32)
    d_hidden = jnp.dot(d_mlp, down_w.T, preferred_element_type=jnp.float32)
    e_pre = d_hidden * gelu_slope(preact)
    d_pre = e_pre.astype(jnp.bfloat16)
    grad_up = jnp.dot(h_two.T, d_pre, preferred_element_type=jnp.float32)
    d_h_two = jnp.dot(d_pre, up_w.T, preferred_element_type=jnp.float32)
    d_scale_two = lax.optimization_barrier(jnp.sum(d_h_two * normed_two, axis=0))
    d_shift_two = lax.optimization_barrier(jnp.sum(d_h_two, axis=0))
    d_mid = upstream + norm_back(normed_two, inv_two, d_h_two * (1.0 + scale_two))
    d_gate_one = lax.optimization_barrier(jnp.sum(d_mid * attn_proj, axis=0))
    e_proj = d_mid * gate_one
    d_proj = e_proj.astype(jnp.bfloat16)
    grad_out = jnp.dot(attn_out.T, d_proj, preferred_element_type=jnp.float32)
    d_attn = jnp.dot(d_proj, out_w.T, preferred_element_type=jnp.float32).astype(jnp.bfloat16)
    queries = qkv_rows[:, :features].reshape(length, HEADS, HD)
    keys_h = qkv_rows[:, features:2 * features].reshape(length, HEADS, HD)
    values_h = qkv_rows[:, 2 * features:].reshape(length, HEADS, HD)
    d_heads = d_attn.reshape(length, HEADS, HD)
    scores = batched('qhd,khd->hqk', queries, keys_h) * HD ** (-0.5)
    prob_again = jnp.exp(scores - log_total[:, :, None])
    d_values = batched('hqk,qhd->khd', prob_again.astype(jnp.bfloat16), d_heads).reshape(length, features)
    d_prob = batched('qhd,khd->hqk', d_heads, values_h)
    row_delta = lax.optimization_barrier(jnp.sum((d_attn.astype(jnp.float32) * attn_out.astype(jnp.float32)).reshape(length, HEADS, HD), axis=-1)).T
    d_scores = (prob_again * (d_prob - row_delta[:, :, None]) * HD ** (-0.5)).astype(jnp.bfloat16)
    d_queries = batched('hqk,khd->qhd', d_scores, keys_h).reshape(length, features)
    d_keys = batched('hqk,qhd->khd', d_scores, queries).reshape(length, features)
    d_qkv = jnp.concatenate([d_queries, d_keys, d_values], axis=1).astype(jnp.bfloat16)
    grad_qkv = jnp.dot(h_one.T, d_qkv, preferred_element_type=jnp.float32)
    d_h_one = jnp.dot(d_qkv, qkv_w.T, preferred_element_type=jnp.float32)
    d_scale_one = lax.optimization_barrier(jnp.sum(d_h_one * normed_one, axis=0))
    d_shift_one = lax.optimization_barrier(jnp.sum(d_h_one, axis=0))
    token_grad = (d_mid + norm_back(normed_one, inv_one, d_h_one * (1.0 + scale_one))).astype(jnp.bfloat16)
    e_mod = jnp.concatenate([d_shift_one, d_scale_one, d_gate_one, d_shift_two, d_scale_two, d_gate_two])
    d_mod = e_mod.astype(jnp.bfloat16)
    grad_mod = activation.astype(jnp.float32)[:, None] * d_mod.astype(jnp.float32)[None, :]
    grad_bias = jnp.concatenate([e_mod, lax.optimization_barrier(jnp.sum(d_queries, axis=0)), lax.optimization_barrier(jnp.sum(d_values, axis=0)), lax.optimization_barrier(jnp.sum(e_proj, axis=0)), lax.optimization_barrier(jnp.sum(e_pre, axis=0)), lax.optimization_barrier(jnp.sum(e_mlp, axis=0))])
    d_act = jnp.dot(d_mod[None, :], mod_w.T, preferred_element_type=jnp.float32)[0]
    cond_full = cond_row.astype(jnp.float32)
    sigmoid_c = jax.nn.sigmoid(cond_full)
    d_cond = d_act * sigmoid_c * (1.0 + cond_full * (1.0 - sigmoid_c))
    return (token_grad, (grad_mod, grad_qkv, grad_out, grad_up, grad_down, grad_bias), d_cond)

def adamw_update(weight, gradient, mean, square):
    mean_new = beta_one * mean + (1.0 - beta_one) * gradient
    square_new = beta_two * square + (1.0 - beta_two) * gradient * gradient
    mean_hat = mean_new / (1.0 - beta_one ** STEP)
    square_hat = square_new / (1.0 - beta_two ** STEP)
    weight_new = weight - learn_rate * (mean_hat / (jnp.sqrt(square_hat) + adam_eps) + weight_decay * weight)
    return (weight_new, mean_new, square_new)

def reference(tokens, cotangent, cond_table, labels, counts, mod_weight, qkv_weight, out_weight, up_weight, down_weight, biases, mod_mean, qkv_mean, out_mean, up_mean, down_mean, bias_mean, mod_square, qkv_square, out_square, up_square, down_square, bias_square):
    masters = (mod_weight, qkv_weight, out_weight, up_weight, down_weight, biases)
    weights = tuple((master.astype(jnp.bfloat16) for master in masters))
    slot_ids = jnp.arange(tokens.shape[0], dtype=jnp.int32)
    live = slot_ids % CAP < counts[slot_ids // CAP]
    class_ids = jnp.arange(CLASSES, dtype=jnp.int32)
    zero_sums = tuple((jnp.zeros(master.shape, jnp.float32) for master in masters)) + (jnp.zeros((CLASSES, tokens.shape[2]), jnp.float32),)

    def latent_step(running, element):
        token_rows, cot_rows, label_id, is_live = element
        cond_row = cond_table[label_id]

        def live_case(sums_in):
            block_value, kept = forward_one(token_rows, cond_row, weights)
            d_tokens, gradients, d_cond = backward_one(cot_rows, cond_row, weights, kept)
            table_term = jnp.where((class_ids == label_id)[:, None], d_cond[None, :], 0.0)
            terms = gradients + (table_term,)
            return (tuple((total + term for total, term in zip(sums_in, terms))), (block_value, d_tokens))

        def dead_case(sums_in):
            return (sums_in, (jnp.zeros_like(token_rows), jnp.zeros_like(token_rows)))
        return lax.cond(is_live, live_case, dead_case, running)
    totals, (block_out, token_grad) = lax.scan(latent_step, zero_sums, (tokens, cotangent, labels, live))
    mod_grad, qkv_grad, out_grad, up_grad, down_grad, bias_grad, table_grad = totals
    mod_next, mean_mod, square_mod = adamw_update(mod_weight, mod_grad, mod_mean, mod_square)
    qkv_next, mean_qkv, square_qkv = adamw_update(qkv_weight, qkv_grad, qkv_mean, qkv_square)
    out_next, mean_out, square_out = adamw_update(out_weight, out_grad, out_mean, out_square)
    up_next, mean_up, square_up = adamw_update(up_weight, up_grad, up_mean, up_square)
    down_next, mean_down, square_down = adamw_update(down_weight, down_grad, down_mean, down_square)
    bias_next, mean_bias, square_bias = adamw_update(biases, bias_grad, bias_mean, bias_square)
    return (block_out, token_grad, table_grad, mod_grad, qkv_grad, out_grad, up_grad, down_grad, bias_grad, mod_next, qkv_next, out_next, up_next, down_next, bias_next, mean_mod, mean_qkv, mean_out, mean_up, mean_down, mean_bias, square_mod, square_qkv, square_out, square_up, square_down, square_bias)
```

```python
import functools

import jax
import jax.numpy as jnp
from jax import lax
from jax.experimental import pallas as pl
from jax.experimental.pallas import tpu as pltpu
from jax.sharding import Mesh
from jax.sharding import PartitionSpec as P

HEADS = 6
HD = 64
STEP = 5


norm_eps = 1e-06
beta_one = 0.9
beta_two = 0.999
adam_eps = 1e-08
learn_rate = 0.01
weight_decay = 0.1
gelu_coef = 0.7978845608
cubic_coef = 0.044715
half = jnp.bfloat16
full = jnp.float32


def dot_nn(left, right):
    return lax.dot_general(left, right, (((1,), (0,)), ((), ())), preferred_element_type=full)


def dot_nt(left, right):
    return lax.dot_general(left, right, (((1,), (1,)), ((), ())), preferred_element_type=full)


def dot_tn(left, right):
    return lax.dot_general(left, right, (((0,), (0,)), ((), ())), preferred_element_type=full)


def layer_norm(values):
    centre = values - jnp.mean(values, axis=-1, keepdims=True)
    inverse = lax.rsqrt(jnp.mean(centre * centre, axis=-1, keepdims=True) + norm_eps)
    return (centre * inverse, inverse)


def norm_back(normed, inverse, upstream):
    return inverse * (
        upstream
        - jnp.mean(upstream, axis=-1, keepdims=True)
        - normed * jnp.mean(upstream * normed, axis=-1, keepdims=True)
    )


def head_masks():
    lane = lax.broadcasted_iota(jnp.int32, (1, 2 * HD), 1)
    low = jnp.where(lane < HD, 1.0, 0.0).astype(full)
    return (low, 1.0 - low)


def load_first(info_ref, weight_ref, parts):
    if len(parts) == 1:
        weight_ref[...] = parts[0][...]
        return
    groups = len(parts) // 2
    rows = parts[0].shape[0]
    for flip in range(2):
        for step in range(groups):
            core = info_ref[1] ^ flip
            group = info_ref[3] ^ step
            top = pl.multiple_of((group * 2 + core) * rows, rows)
            weight_ref[pl.ds(top, rows), :] = parts[flip * groups + step][...]


def load_second(info_ref, up_ref, down_ref, parts):
    width = up_ref.shape[2]
    if parts[0].ndim == 2:
        for chunk in range(up_ref.shape[0]):
            up_ref[chunk] = parts[0][:, chunk * width : (chunk + 1) * width]
        down_ref[...] = parts[1][...]
        return
    chips = len(parts) // 2
    groups, _, rows, _ = parts[0].shape
    for flip in range(2):
        for hop in range(chips):
            for step in range(groups):
                core = info_ref[1] ^ flip
                chip = info_ref[2] ^ hop
                group = info_ref[3] ^ step
                source = parts[flip * chips + hop]
                top = pl.multiple_of((group * 2 + core) * rows, rows)
                up_ref[chip, pl.ds(top, rows), :] = source[step, 0]
                top = pl.multiple_of(((group * chips + chip) * 2 + core) * rows, rows)
                down_ref[pl.ds(top, rows), :] = source[step, 1]


def attn_forward(info_ref, tok_ref, mod_ref, bias_ref, *rest):
    *parts, qkv_ref, prob_ref, attn_ref, proj_ref, weight_ref = rest
    features = tok_ref.shape[2]

    @pl.when(pl.program_id(0) == 0)
    def _():
        load_first(info_ref, weight_ref, parts)

    @pl.when(pl.program_id(0) < info_ref[0])
    def _():
        mods = mod_ref[0]
        shift_one = mods[:, :features]
        scale_one = mods[:, features : 2 * features]
        inputs = tok_ref[0].astype(full)
        normed_one, _ = layer_norm(inputs)
        h_one = (normed_one * (1.0 + scale_one) + shift_one).astype(half)
        masks = head_masks()
        qkv_ref[0] = (
            dot_nn(h_one, weight_ref[:, : 3 * features]) + bias_ref[:, : 3 * features]
        ).astype(half)
        width = 2 * HD
        for pair in range(HEADS // 2):
            low = pair * width
            queries = qkv_ref[0, :, low : low + width]
            keys_h = qkv_ref[0, :, features + low : features + low + width]
            values_h = qkv_ref[0, :, 2 * features + low : 2 * features + low + width]
            total = None
            for side in range(2):
                scaled = queries * (masks[side] * HD ** (-0.5)).astype(half)
                exponent = jnp.exp(dot_nt(scaled, keys_h))
                row_total = jnp.sum(exponent, axis=-1, keepdims=True)
                probs = (exponent * (1.0 / row_total)).astype(half)
                prob_ref[0, 2 * pair + side] = probs
                term = dot_nn(probs, values_h * masks[side].astype(half))
                total = term if total is None else total + term
            attn_ref[0, :, low : low + width] = total.astype(half)
        proj_ref[0] = (
            dot_nn(attn_ref[0], weight_ref[:, 3 * features :]) + bias_ref[:, 3 * features :]
        )


def mlp_both(count_parts, info_ref, tok_ref, cot_ref, mod_ref, proj_ref, bias_ref, *rest):
    features = tok_ref.shape[2]
    parts = rest[:count_parts]
    out_ref, dmid_ref, keep_ref, send_ref, note_ref, *rest = rest[count_parts:]
    vec_ref, hidden_ref, slope_ref, acc_up, acc_down, down_t, up_ref, down_ref = rest
    wide = hidden_ref.shape[1]
    slot = pl.program_id(0)
    chunks = wide // features

    @pl.when(slot == 0)
    def _():
        load_second(info_ref, up_ref, down_ref, parts)
        acc_up[...] = jnp.zeros_like(acc_up)
        acc_down[...] = jnp.zeros_like(acc_down)
        vec_ref[...] = jnp.zeros_like(vec_ref)

    @pl.when(slot >= info_ref[0])
    def _():
        out_ref[...] = jnp.zeros_like(out_ref)

    @pl.when(slot < info_ref[0])
    def _():
        mods = mod_ref[0]
        gate_one = mods[:, 2 * features : 3 * features]
        shift_two = mods[:, 3 * features : 4 * features]
        scale_two = mods[:, 4 * features : 5 * features]
        gate_two = mods[:, 5 * features :]
        residual = tok_ref[0].astype(full) + gate_one * proj_ref[0]
        normed_two, inv_two = layer_norm(residual)
        h_two = (normed_two * (1.0 + scale_two) + shift_two).astype(half)
        mlp = None
        for j in range(chunks):
            cols = slice(j * features, (j + 1) * features)
            pre = dot_nn(h_two, up_ref[j]) + bias_ref[:, cols]
            square = pre * pre
            tanh_value = jnp.tanh(pre * (gelu_coef + gelu_coef * cubic_coef * square))
            gate = 0.5 + 0.5 * tanh_value
            hidden = pre * gate
            slope_ref[:, cols] = gate + hidden * (1.0 - gate) * (
                2.0 * gelu_coef + 6.0 * gelu_coef * cubic_coef * square
            )
            hidden_ref[:, cols] = hidden.astype(half)
            term = dot_nn(hidden_ref[:, cols], down_ref[cols, :])
            mlp = term if mlp is None else mlp + term
        mlp = mlp + bias_ref[:, wide:]
        out_ref[0] = (residual + gate_two * mlp).astype(half)
        upstream = cot_ref[0].astype(full)
        d_gate_two = jnp.sum(upstream * mlp, axis=0, keepdims=True)
        e_mlp = upstream * gate_two
        sum_mlp = jnp.sum(e_mlp, axis=0, keepdims=True)
        d_mlp = e_mlp.astype(half)
        d_h_two = None
        for j in range(chunks):
            cols = slice(j * features, (j + 1) * features)
            acc_down[:, cols] += dot_tn(d_mlp, hidden_ref[:, cols])
            e_pre = dot_nt(d_mlp, down_ref[cols, :]) * slope_ref[:, cols]
            vec_ref[4:5, cols] += jnp.sum(e_pre, axis=0, keepdims=True)
            d_pre = e_pre.astype(half)
            acc_up[j] += dot_tn(h_two, d_pre)
            term = dot_nt(d_pre, up_ref[j])
            d_h_two = term if d_h_two is None else d_h_two + term
        d_scale_two = jnp.sum(d_h_two * normed_two, axis=0, keepdims=True)
        d_shift_two = jnp.sum(d_h_two, axis=0, keepdims=True)
        d_mid = upstream + norm_back(normed_two, inv_two, d_h_two * (1.0 + scale_two))
        d_gate_one = jnp.sum(d_mid * proj_ref[0], axis=0, keepdims=True)
        sum_proj = jnp.sum(d_mid, axis=0, keepdims=True) * gate_one
        dmid_ref[0] = d_mid
        vec_ref[5:6, :features] += sum_proj
        vec_ref[5:6, features : 2 * features] += sum_mlp
        vec_ref[pl.ds(slot, 1), :] = jnp.concatenate(
            [d_gate_one, d_shift_two, d_scale_two, d_gate_two], axis=1
        )

    @pl.when(slot == pl.num_programs(0) - 1)
    def _():
        lane = lax.broadcasted_iota(jnp.int32, (1, wide), 1)
        codes = jnp.zeros((1, wide), full)
        for row in range(8):
            label = info_ref[4 + row]
            high = (label >> 5).astype(full)
            low = (label & 31).astype(full)
            codes = jnp.where(lane == row, high, codes)
            codes = jnp.where(lane == 8 + row, low, codes)
        vec_ref[6:7, :] = codes
        note_ref[...] = vec_ref[...].astype(half)
        if keep_ref.ndim == 2:
            for j in range(chunks):
                keep_ref[:, j * features : (j + 1) * features] = acc_up[j].astype(half)
            send_ref[...] = acc_down[...].T.astype(half)
            return
        down_t[...] = acc_down[...].T
        chips, groups, _, rows, _ = keep_ref.shape
        for flip, target in enumerate((keep_ref, send_ref)):
            core = info_ref[1] ^ flip
            for hop in range(chips):
                for step in range(groups):
                    chip = info_ref[2] ^ hop
                    group = info_ref[3] ^ step
                    top = pl.multiple_of((group * 2 + core) * rows, rows)
                    target[hop, step, 0] = acc_up[chip, pl.ds(top, rows), :].astype(half)
                    top = pl.multiple_of(((group * chips + chip) * 2 + core) * rows, rows)
                    target[hop, step, 1] = down_t[pl.ds(top, rows), :].astype(half)


def attn_backward(info_ref, tok_ref, mod_ref, qkv_ref, prob_ref, attn_ref, dmid_ref, *rest):
    *parts, grad_ref, keep_ref, send_ref, note_ref, vec_ref, d_qkv_ref, acc_ref, weight_ref = rest
    features = tok_ref.shape[2]
    slot = pl.program_id(0)

    @pl.when(slot == 0)
    def _():
        load_first(info_ref, weight_ref, parts)
        acc_ref[...] = jnp.zeros_like(acc_ref)
        vec_ref[...] = jnp.zeros_like(vec_ref)

    @pl.when(slot >= info_ref[0])
    def _():
        grad_ref[...] = jnp.zeros_like(grad_ref)

    @pl.when(slot < info_ref[0])
    def _():
        mods = mod_ref[0]
        shift_one = mods[:, :features]
        scale_one = mods[:, features : 2 * features]
        gate_one = mods[:, 2 * features : 3 * features]
        normed_one, inv_one = layer_norm(tok_ref[0].astype(full))
        h_one = (normed_one * (1.0 + scale_one) + shift_one).astype(half)
        d_mid = dmid_ref[0]
        d_proj = (d_mid * gate_one).astype(half)
        acc_ref[:, 3 * features :] += dot_tn(attn_ref[0], d_proj)
        d_attn = dot_nt(d_proj, weight_ref[:, 3 * features :]).astype(half)
        masks = head_masks()
        width = 2 * HD
        for pair in range(HEADS // 2):
            low = pair * width
            queries = qkv_ref[0, :, low : low + width]
            keys_h = qkv_ref[0, :, features + low : features + low + width]
            values_h = qkv_ref[0, :, 2 * features + low : 2 * features + low + width]
            d_heads = d_attn[:, low : low + width]
            product = d_heads.astype(full) * attn_ref[0, :, low : low + width].astype(full)
            sums = [None, None, None]
            for side in range(2):
                mask = masks[side]
                probs = prob_ref[0, 2 * pair + side]
                d_side = d_heads * mask.astype(half)
                delta = jnp.sum(product * mask, axis=-1, keepdims=True)
                d_prob = dot_nt(d_side, values_h)
                d_scores = (probs.astype(full) * (d_prob - delta)).astype(half)
                scaled = (mask * HD ** (-0.5)).astype(half)
                terms = (
                    dot_nn(d_scores, keys_h * scaled),
                    dot_tn(d_scores, queries * scaled),
                    dot_tn(probs, d_side),
                )
                sums = [
                    term if total is None else total + term for total, term in zip(sums, terms)
                ]
            for part in range(3):
                d_qkv_ref[:, part * features + low : part * features + low + width] = sums[
                    part
                ].astype(half)
            vec_ref[4:5, low : low + width] += jnp.sum(sums[0], axis=0, keepdims=True)
            vec_ref[4:5, features + low : features + low + width] += jnp.sum(
                sums[2], axis=0, keepdims=True
            )
        acc_ref[:, : 3 * features] += dot_tn(h_one, d_qkv_ref[...])
        d_h_one = dot_nt(d_qkv_ref[...], weight_ref[:, : 3 * features])
        d_scale_one = jnp.sum(d_h_one * normed_one, axis=0, keepdims=True)
        d_shift_one = jnp.sum(d_h_one, axis=0, keepdims=True)
        grad_ref[0] = (d_mid + norm_back(normed_one, inv_one, d_h_one * (1.0 + scale_one))).astype(
            half
        )
        vec_ref[pl.ds(slot, 1), :] = jnp.concatenate([d_shift_one, d_scale_one], axis=1)

    @pl.when(slot == pl.num_programs(0) - 1)
    def _():
        note_ref[...] = vec_ref[...].astype(half)
        if keep_ref.ndim == 2:
            keep_ref[...] = acc_ref[...].astype(half)
            send_ref[...] = jnp.zeros_like(send_ref)
            return
        pieces, rows, cols = keep_ref.shape
        chips = acc_ref.shape[1] // cols
        groups = pieces // chips
        for flip, target in enumerate((keep_ref, send_ref)):
            core = info_ref[1] ^ flip
            for chip in range(chips):
                for group in range(groups):
                    top = pl.multiple_of((group * 2 + core) * rows, rows)
                    target[chip * groups + group] = acc_ref[
                        pl.ds(top, rows), chip * cols : (chip + 1) * cols
                    ].astype(half)


def per_slot(*extent):
    return pl.BlockSpec((1,) + extent, lambda slot, info: (slot,) + (0,) * len(extent))


def whole(*extent):
    return pl.BlockSpec(extent, lambda slot, info: (0,) * len(extent))


def run_kernel(kernel, steps, work, ins, outs, scratch, info, operands):
    return pl.pallas_call(
        kernel,
        grid_spec=pltpu.PrefetchScalarGridSpec(
            num_scalar_prefetch=1,
            grid=(steps,),
            in_specs=ins,
            out_specs=[spec for spec, _ in outs],
            scratch_shapes=scratch,
        ),
        out_shape=[shape for _, shape in outs],
        cost_estimate=pl.CostEstimate(
            flops=int(work), bytes_accessed=int(work) // 300, transcendentals=int(work) // 1000
        ),
    )(info, *operands)


def adamw_update(weight, gradient, mean, square):
    mean_new = beta_one * mean + (1.0 - beta_one) * gradient
    square_new = beta_two * square + (1.0 - beta_two) * gradient * gradient
    mean_hat = mean_new / (1.0 - beta_one**STEP)
    square_hat = square_new / (1.0 - beta_two**STEP)
    weight_new = weight - learn_rate * (
        mean_hat / (jnp.sqrt(square_hat) + adam_eps) + weight_decay * weight
    )
    return (weight_new, mean_new, square_new)


def swap(values, axis, step):
    count = lax.axis_size(axis)
    return lax.ppermute(values, axis, [(i, i ^ step) for i in range(count)])


def exchange(pieces, axes):
    return lax.all_to_all(pieces, axes, 0, 0, tiled=True)


def spread(values, count, axes):
    return exchange(jnp.broadcast_to(values[None], (count,) + values.shape), axes)


def neighbours(values, axis):
    return [values] + [swap(values, axis, k) for k in range(1, lax.axis_size(axis))]


def order(pieces, index):
    buffer = jnp.zeros((len(pieces),) + pieces[0].shape, pieces[0].dtype)
    for step, piece in enumerate(pieces):
        buffer = lax.dynamic_update_index_in_dim(buffer, piece, index ^ step, 0)
    return buffer


def choose(values, index):
    return lax.dynamic_index_in_dim(values, index, 0, keepdims=False)


def add_up(pieces):
    return jnp.sum(pieces.astype(full), axis=0)


def body(
    reps,
    groups,
    tokens,
    cotangent,
    cond_table,
    labels,
    counts,
    mod_weight,
    qkv_weight,
    out_weight,
    up_weight,
    down_weight,
    biases,
    mod_mean,
    qkv_mean,
    out_mean,
    up_mean,
    down_mean,
    bias_mean,
    mod_square,
    qkv_square,
    out_square,
    up_square,
    down_square,
    bias_square,
):
    cores = 2
    chips = reps // cores
    devices = reps * groups
    core = lax.axis_index("core")
    chip = lax.axis_index("chip")
    group = lax.axis_index("fsdp")
    capacity, length, features = tokens.shape
    classes_all = cond_table.shape[0]
    wide = up_weight.shape[1]
    shard = features // groups
    rows = shard // cores
    cols = wide // chips
    down_rows = wide // (devices)
    aligned = rows % 16 == 0 and cols % 128 == 0 and (rows, cols) == (down_rows, features)

    live = lax.iota(jnp.int32, capacity) < counts[0]
    own_labels = jnp.where(live, labels, -1)
    head = jnp.concatenate([own_labels.astype(full), lax.reduce_precision(biases, 8, 7)])
    heads = spread(head[None], groups, "fsdp")[:, 0]
    group_labels = heads[:, :capacity].astype(jnp.int32)
    bias_full = heads[:, capacity:].reshape(-1)

    first_own = jnp.concatenate(
        [
            lax.dynamic_slice_in_dim(qkv_weight, core * rows, rows, 0),
            lax.dynamic_slice_in_dim(out_weight, core * rows, rows, 0),
        ],
        axis=1,
    ).astype(half)
    first_own = neighbours(first_own, "fsdp")
    first_other = [swap(part, "core", 1) for part in first_own]

    second_up = lax.dynamic_slice(up_weight, (core * rows, chip * cols), (rows, cols))
    second_down = lax.dynamic_slice_in_dim(
        down_weight, (chip * cores + core) * down_rows, down_rows, 0
    )
    if aligned:
        second_own = jnp.stack([second_up, second_down])
    else:
        second_own = jnp.concatenate([second_up.reshape(-1), second_down.reshape(-1)])
    second_own = jnp.stack(neighbours(second_own.astype(half), "fsdp"))
    second_own = neighbours(second_own, "chip")

    mod_half = mod_weight.astype(half)
    column = group * shard
    group_cond = cond_table[jnp.maximum(group_labels.reshape(-1), 0)]
    group_cond = lax.dynamic_slice_in_dim(group_cond, column, shard, 1).astype(full)
    partial = jnp.dot(
        jax.nn.silu(group_cond).astype(half), mod_half, preferred_element_type=full
    ).reshape(groups, capacity, 6 * features)
    modulation = add_up(exchange(partial, "fsdp")) + bias_full[: 6 * features]
    modulation = modulation[:, None, :]

    if aligned:
        first_parts = first_own + first_other
    else:
        first_all = order([order(first_own, group), order(first_other, group)], core)
        first_parts = [first_all.transpose(1, 0, 2, 3).reshape(features, wide)]

    info = jnp.concatenate(
        [
            jnp.stack([counts[0], core, chip, group]).astype(jnp.int32),
            own_labels,
            jnp.full((8 - capacity,), -1, jnp.int32),
        ]
    )
    nothing = jnp.zeros((features,), full)
    b0 = 6 * features
    first_bias = jnp.concatenate(
        [
            bias_full[b0 : b0 + features],
            nothing,
            bias_full[b0 + features : b0 + 3 * features],
        ]
    )[None]
    second_bias = bias_full[b0 + 3 * features :][None]
    slot_tok = per_slot(length, features)
    slot_mod = per_slot(1, 6 * features)
    first_specs = [whole(*part.shape) for part in first_parts]
    work = 2 * capacity * length * features * wide * 4

    def shaped(dtype, *extent):
        return jax.ShapeDtypeStruct(extent, dtype)

    qkv_rows, probs, attn_out, proj = run_kernel(
        attn_forward,
        capacity,
        2 * work,
        [slot_tok, slot_mod, whole(1, wide), *first_specs],
        [
            (per_slot(length, 3 * features), shaped(half, capacity, length, 3 * features)),
            (per_slot(HEADS, length, length), shaped(half, capacity, HEADS, length, length)),
            (slot_tok, shaped(half, capacity, length, features)),
            (slot_tok, shaped(full, capacity, length, features)),
        ],
        [pltpu.VMEM((features, wide), half)],
        info,
        (tokens, modulation, first_bias, *first_parts),
    )

    second_own, proj = lax.optimization_barrier((second_own, proj))
    second_other = [swap(part, "core", 1) for part in second_own]
    if aligned:
        second_parts = second_own + second_other
    else:
        second_all = order(
            [
                order([order(list(part), group) for part in side], chip)
                for side in (second_own, second_other)
            ],
            core,
        )
        border = rows * cols
        second_parts = [
            second_all[..., :border]
            .reshape(cores, chips, groups, rows, cols)
            .transpose(2, 0, 3, 1, 4)
            .reshape(features, wide),
            second_all[..., border:]
            .reshape(cores, chips, groups, down_rows, features)
            .transpose(2, 1, 0, 3, 4)
            .reshape(wide, features),
        ]
    second_specs = [whole(*part.shape) for part in second_parts]

    if aligned:
        first_packs = [(chips * groups, rows, cols)] * 2
        second_packs = [(chips, groups, 2, rows, cols)] * 2
    else:
        first_packs = [(features, wide), (8, 128)]
        second_packs = [(features, wide), (wide, features)]
    block_out, d_mid, second_keep, second_send, note_two = run_kernel(
        functools.partial(mlp_both, len(second_parts)),
        capacity,
        4 * work,
        [
            slot_tok,
            slot_tok,
            slot_mod,
            slot_tok,
            whole(1, wide + features),
            *second_specs,
        ],
        [
            (slot_tok, shaped(half, capacity, length, features)),
            (slot_tok, shaped(full, capacity, length, features)),
            *[(whole(*pack), shaped(half, *pack)) for pack in second_packs],
            (whole(8, wide), shaped(half, 8, wide)),
        ],
        [
            pltpu.VMEM((8, wide), full),
            pltpu.VMEM((length, wide), half),
            pltpu.VMEM((length, wide), full),
            pltpu.VMEM((wide // features, features, features), full),
            pltpu.VMEM((features, wide), full),
            pltpu.VMEM((wide, features), full),
            pltpu.VMEM((wide // features, features, features), half),
            pltpu.VMEM((wide, features), half),
        ],
        info,
        (tokens, cotangent, modulation, proj, second_bias, *second_parts),
    )
    if not aligned:
        up_part = (
            second_keep.reshape(groups, cores, rows, chips, cols)
            .transpose(1, 3, 0, 2, 4)
            .reshape(cores, chips, groups, -1)
        )
        down_part = (
            second_send.reshape(groups, chips, cores, down_rows, features)
            .transpose(2, 1, 0, 3, 4)
            .reshape(cores, chips, groups, -1)
        )
        packed = jnp.concatenate([up_part, down_part], axis=-1)
        packed = packed[:, lax.iota(jnp.int32, chips) ^ chip]
        packed = packed[:, :, lax.iota(jnp.int32, groups) ^ group]
        second_keep, second_send = choose(packed, core), choose(packed, 1 - core)
    second_back = swap(second_send, "core", 1)
    by_chip = [
        (second_keep[k].astype(full) + second_back[k].astype(full)).astype(half)
        for k in range(chips)
    ]
    by_chip = [by_chip[0]] + [swap(by_chip[k], "chip", k) for k in range(1, chips)]
    all_two = spread(note_two, devices, ("chip", "core", "fsdp"))

    token_grad, first_keep, first_send, note_three = run_kernel(
        attn_backward,
        capacity,
        3 * work,
        [
            slot_tok,
            slot_mod,
            per_slot(length, 3 * features),
            per_slot(HEADS, length, length),
            slot_tok,
            slot_tok,
            *first_specs,
        ],
        [
            (slot_tok, shaped(half, capacity, length, features)),
            *[(whole(*pack), shaped(half, *pack)) for pack in first_packs],
            (whole(8, 2 * features), shaped(half, 8, 2 * features)),
        ],
        [
            pltpu.VMEM((8, 2 * features), full),
            pltpu.VMEM((length, 3 * features), half),
            pltpu.VMEM((features, wide), full),
            pltpu.VMEM((features, wide), half),
        ],
        info,
        (tokens, modulation, qkv_rows, probs, attn_out, d_mid, *first_parts),
    )
    if not aligned:
        packed = (
            first_keep.reshape(groups, cores, rows, chips, cols)
            .transpose(1, 3, 0, 2, 4)
            .reshape(cores, chips * groups, rows, cols)
        )
        first_keep, first_send = choose(packed, core), choose(packed, 1 - core)
    first_back = swap(first_send, "core", 1)
    first_sum = (first_keep.astype(full) + first_back.astype(full)).astype(half)
    pieces = exchange(first_sum, ("chip", "fsdp"))
    by_chip, all_two, first_sum = lax.optimization_barrier((by_chip, all_two, first_sum))

    by_group = []
    for k in range(groups):
        total = by_chip[0][k].astype(full)
        for part in by_chip[1:]:
            total = total + part[k].astype(full)
        by_group.append(total.astype(half))
    second_sum = by_group[0].astype(full)
    for k in range(1, groups):
        second_sum = second_sum + swap(by_group[k], "fsdp", k).astype(full)
    second_sum = second_sum.astype(half)

    note_three = jnp.stack(neighbours(note_three, "fsdp"))
    note_three = jnp.stack(neighbours(note_three, "chip"))
    note_three = jnp.stack(neighbours(note_three, "core"))
    count = devices * 8
    spot = lax.iota(jnp.int32, count)
    line, where = spot % 8, spot // 8
    where_group = (where % groups) ^ group
    where_core = (where // groups % cores) ^ core
    where_chip = (where // (groups * cores)) ^ chip
    where = ((where_core * chips + where_chip) * groups + where_group) * 8 + line
    moved = (where[:, None] == spot[None, :]).astype(half)
    d_three = jnp.dot(
        moved, note_three.reshape(count, 2 * features), preferred_element_type=full
    ).astype(half)
    d_two = all_two.reshape(count, wide)

    first_sum = add_up(pieces).astype(half)
    if aligned:
        third = jnp.concatenate([second_sum, first_sum[None]])
    else:
        third = jnp.concatenate([second_sum, first_sum.reshape(-1)])
    third = spread(third, reps, ("chip", "core")).reshape(chips, cores, *third.shape)
    if aligned:
        up_all, down_all, first_all = third[:, :, 0], third[:, :, 1], third[:, :, 2]
    else:
        border = rows * cols
        up_all = third[..., :border].reshape(chips, cores, rows, cols)
        down_all = third[..., border : border + down_rows * features]
        first_all = third[..., border + down_rows * features :]
        first_all = first_all.reshape(chips, cores, rows, cols)
    up_grad = up_all.transpose(1, 2, 0, 3).reshape(shard, wide).astype(full)
    down_grad = down_all.reshape(down_weight.shape).astype(full)
    first_grad = first_all.transpose(1, 2, 0, 3).reshape(shard, wide).astype(full)
    qkv_grad = first_grad[:, : 3 * features]
    out_grad = first_grad[:, 3 * features :]

    label_notes = all_two[:, 6, :16].astype(jnp.int32)
    all_labels = (32 * label_notes[:, :8] + label_notes[:, 8:]).reshape(-1)
    all_cond = cond_table[jnp.maximum(all_labels, 0)]
    all_cond = lax.dynamic_slice_in_dim(all_cond, column, shard, 1).astype(full)
    all_live = (all_labels >= 0)[:, None]
    sigmoid_c = jax.nn.sigmoid(all_cond)
    all_active = jnp.where(all_live, all_cond * sigmoid_c, 0.0).astype(half)
    slope_c = jnp.where(all_live, sigmoid_c * (1.0 + all_cond * (1.0 - sigmoid_c)), 0.0)
    mod_grad = jnp.concatenate([dot_tn(all_active, d_three), dot_tn(all_active, d_two)], axis=1)
    d_act = dot_nt(d_three, mod_half[:, : 2 * features]) + dot_nt(
        d_two, mod_half[:, 2 * features :]
    )
    picks = jnp.stack([line < capacity, line == 4, line == 5]).astype(half)
    sum_two = dot_nn(picks, d_two)
    sum_three = dot_nn(picks, d_three)
    d_cond = order(neighbours((d_act * slope_c).astype(half), "fsdp"), group)
    class_share = classes_all // groups
    class_ids = lax.iota(jnp.int32, class_share) + group * class_share
    chosen = (class_ids[:, None] == all_labels[None, :]).astype(half)
    table_grad = jnp.concatenate(
        [
            jnp.dot(chosen, d_cond[k], preferred_element_type=full)
            for k in range(groups)
        ],
        axis=1,
    )
    bias_all = jnp.concatenate(
        [
            sum_three[0],
            sum_two[0],
            sum_three[1],
            sum_two[2, :features],
            sum_two[1],
            sum_two[2, features : 2 * features],
        ]
    )
    bias_share = biases.shape[0]
    bias_grad = lax.dynamic_slice_in_dim(bias_all, group * bias_share, bias_share, 0)

    mod_next, mean_mod, square_mod = adamw_update(mod_weight, mod_grad, mod_mean, mod_square)
    qkv_next, mean_qkv, square_qkv = adamw_update(qkv_weight, qkv_grad, qkv_mean, qkv_square)
    out_next, mean_out, square_out = adamw_update(out_weight, out_grad, out_mean, out_square)
    up_next, mean_up, square_up = adamw_update(up_weight, up_grad, up_mean, up_square)
    down_next, mean_down, square_down = adamw_update(down_weight, down_grad, down_mean, down_square)
    bias_next, mean_bias, square_bias = adamw_update(biases, bias_grad, bias_mean, bias_square)
    return (
        block_out,
        token_grad,
        table_grad,
        mod_grad,
        qkv_grad,
        out_grad,
        up_grad,
        down_grad,
        bias_grad,
        mod_next,
        qkv_next,
        out_next,
        up_next,
        down_next,
        bias_next,
        mean_mod,
        mean_qkv,
        mean_out,
        mean_up,
        mean_down,
        mean_bias,
        square_mod,
        square_qkv,
        square_out,
        square_up,
        square_down,
        square_bias,
    )


def solution(mesh):
    placed = (
        P(("chip", "core", "fsdp"), None, None),
        P(("chip", "core", "fsdp"), None, None),
        P(),
        P(("chip", "core", "fsdp")),
        P(("chip", "core", "fsdp")),
        P("fsdp", None),
        P("fsdp", None),
        P("fsdp", None),
        P("fsdp", None),
        P("fsdp", None),
        P("fsdp"),
        P("fsdp", None),
        P("fsdp", None),
        P("fsdp", None),
        P("fsdp", None),
        P("fsdp", None),
        P("fsdp"),
        P("fsdp", None),
        P("fsdp", None),
        P("fsdp", None),
        P("fsdp", None),
        P("fsdp", None),
        P("fsdp"),
    )
    reps, groups = mesh.shape["rep"], mesh.shape["fsdp"]
    fine = Mesh(mesh.devices.reshape(reps // 2, 2, groups), ("chip", "core", "fsdp"))
    return jax.shard_map(
        functools.partial(body, reps, groups),
        mesh=fine,
        in_specs=placed,
        out_specs=(
            P(("chip", "core", "fsdp"), None, None),
            P(("chip", "core", "fsdp"), None, None),
            P("fsdp", None),
            P("fsdp", None),
            P("fsdp", None),
            P("fsdp", None),
            P("fsdp", None),
            P("fsdp", None),
            P("fsdp"),
            P("fsdp", None),
            P("fsdp", None),
            P("fsdp", None),
            P("fsdp", None),
            P("fsdp", None),
            P("fsdp"),
            P("fsdp", None),
            P("fsdp", None),
            P("fsdp", None),
            P("fsdp", None),
            P("fsdp", None),
            P("fsdp"),
            P("fsdp", None),
            P("fsdp", None),
            P("fsdp", None),
            P("fsdp", None),
            P("fsdp", None),
            P("fsdp"),
        ),
        check_vma=False,
    )
```

```python
import functools

import jax
import jax.numpy as jnp
from jax import lax
from jax.experimental import pallas as pl
from jax.experimental.pallas import tpu as pltpu
from jax.sharding import Mesh
from jax.sharding import PartitionSpec as P

HEADS = 6
HD = 64
STEP = 5


norm_eps = 1e-06
beta_one = 0.9
beta_two = 0.999
adam_eps = 1e-08
learn_rate = 0.01
weight_decay = 0.1
gelu_coef = 0.7978845608
cubic_coef = 0.044715
half = jnp.bfloat16
full = jnp.float32


def dot_nn(left, right):
    return lax.dot_general(left, right, (((1,), (0,)), ((), ())), preferred_element_type=full)


def dot_nt(left, right):
    return lax.dot_general(left, right, (((1,), (1,)), ((), ())), preferred_element_type=full)


def dot_tn(left, right):
    return lax.dot_general(left, right, (((0,), (0,)), ((), ())), preferred_element_type=full)


def layer_norm(values):
    centre = values - jnp.mean(values, axis=-1, keepdims=True)
    inverse = lax.rsqrt(jnp.mean(centre * centre, axis=-1, keepdims=True) + norm_eps)
    return (centre * inverse, inverse)


def norm_back(normed, inverse, upstream):
    return inverse * (
        upstream
        - jnp.mean(upstream, axis=-1, keepdims=True)
        - normed * jnp.mean(upstream * normed, axis=-1, keepdims=True)
    )


def head_masks():
    lane = lax.broadcasted_iota(jnp.int32, (1, 2 * HD), 1)
    low = jnp.where(lane < HD, 1.0, 0.0).astype(full)
    return (low, 1.0 - low)


def load_first(info_ref, weight_ref, parts):
    if len(parts) == 1:
        weight_ref[...] = parts[0][...]
        return
    groups = len(parts) // 2
    rows = parts[0].shape[0]
    for flip in range(2):
        for step in range(groups):
            core = info_ref[1] ^ flip
            group = info_ref[3] ^ step
            top = pl.multiple_of((group * 2 + core) * rows, rows)
            weight_ref[pl.ds(top, rows), :] = parts[flip * groups + step][...]


def load_second(info_ref, up_ref, down_ref, parts):
    width = up_ref.shape[2]
    if parts[0].ndim == 2:
        for chunk in range(up_ref.shape[0]):
            up_ref[chunk] = parts[0][:, chunk * width : (chunk + 1) * width]
        down_ref[...] = parts[1][...]
        return
    chips = len(parts) // 2
    groups, _, rows, _ = parts[0].shape
    for flip in range(2):
        for hop in range(chips):
            for step in range(groups):
                core = info_ref[1] ^ flip
                chip = info_ref[2] ^ hop
                group = info_ref[3] ^ step
                source = parts[flip * chips + hop]
                top = pl.multiple_of((group * 2 + core) * rows, rows)
                up_ref[chip, pl.ds(top, rows), :] = source[step, 0]
                top = pl.multiple_of(((group * chips + chip) * 2 + core) * rows, rows)
                down_ref[pl.ds(top, rows), :] = source[step, 1]


def attn_forward(info_ref, tok_ref, mod_ref, bias_ref, *rest):
    *parts, qkv_ref, prob_ref, attn_ref, proj_ref, weight_ref = rest
    features = tok_ref.shape[2]

    @pl.when(pl.program_id(0) == 0)
    def _():
        load_first(info_ref, weight_ref, parts)

    @pl.when(pl.program_id(0) < info_ref[0])
    def _():
        mods = mod_ref[0]
        shift_one = mods[:, :features]
        scale_one = mods[:, features : 2 * features]
        inputs = tok_ref[0].astype(full)
        normed_one, _ = layer_norm(inputs)
        h_one = (normed_one * (1.0 + scale_one) + shift_one).astype(half)
        masks = head_masks()
        qkv_ref[0] = (
            dot_nn(h_one, weight_ref[:, : 3 * features]) + bias_ref[:, : 3 * features]
        ).astype(half)
        width = 2 * HD
        for pair in range(HEADS // 2):
            low = pair * width
            queries = qkv_ref[0, :, low : low + width]
            keys_h = qkv_ref[0, :, features + low : features + low + width]
            values_h = qkv_ref[0, :, 2 * features + low : 2 * features + low + width]
            total = None
            for side in range(2):
                scaled = queries * (masks[side] * HD ** (-0.5)).astype(half)
                exponent = jnp.exp(dot_nt(scaled, keys_h))
                row_total = jnp.sum(exponent, axis=-1, keepdims=True)
                probs = (exponent * (1.0 / row_total)).astype(half)
                prob_ref[0, 2 * pair + side] = probs
                term = dot_nn(probs, values_h * masks[side].astype(half))
                total = term if total is None else total + term
            attn_ref[0, :, low : low + width] = total.astype(half)
        proj_ref[0] = (
            dot_nn(attn_ref[0], weight_ref[:, 3 * features :]) + bias_ref[:, 3 * features :]
        )


def mlp_both(count_parts, info_ref, tok_ref, cot_ref, mod_ref, proj_ref, bias_ref, *rest):
    features = tok_ref.shape[2]
    parts = rest[:count_parts]
    out_ref, dmid_ref, keep_ref, send_ref, note_ref, *rest = rest[count_parts:]
    vec_ref, hidden_ref, slope_ref, acc_up, acc_down, down_t, up_ref, down_ref = rest
    wide = hidden_ref.shape[1]
    slot = pl.program_id(0)
    chunks = wide // features

    @pl.when(slot == 0)
    def _():
        load_second(info_ref, up_ref, down_ref, parts)
        acc_up[...] = jnp.zeros_like(acc_up)
        acc_down[...] = jnp.zeros_like(acc_down)
        vec_ref[...] = jnp.zeros_like(vec_ref)

    @pl.when(slot >= info_ref[0])
    def _():
        out_ref[...] = jnp.zeros_like(out_ref)

    @pl.when(slot < info_ref[0])
    def _():
        mods = mod_ref[0]
        gate_one = mods[:, 2 * features : 3 * features]
        shift_two = mods[:, 3 * features : 4 * features]
        scale_two = mods[:, 4 * features : 5 * features]
        gate_two = mods[:, 5 * features :]
        residual = tok_ref[0].astype(full) + gate_one * proj_ref[0]
        normed_two, inv_two = layer_norm(residual)
        h_two = (normed_two * (1.0 + scale_two) + shift_two).astype(half)
        mlp = None
        for j in range(chunks):
            cols = slice(j * features, (j + 1) * features)
            pre = dot_nn(h_two, up_ref[j]) + bias_ref[:, cols]
            square = pre * pre
            tanh_value = jnp.tanh(pre * (gelu_coef + gelu_coef * cubic_coef * square))
            gate = 0.5 + 0.5 * tanh_value
            hidden = pre * gate
            slope_ref[:, cols] = gate + hidden * (1.0 - gate) * (
                2.0 * gelu_coef + 6.0 * gelu_coef * cubic_coef * square
            )
            hidden_ref[:, cols] = hidden.astype(half)
            term = dot_nn(hidden_ref[:, cols], down_ref[cols, :])
            mlp = term if mlp is None else mlp + term
        mlp = mlp + bias_ref[:, wide:]
        out_ref[0] = (residual + gate_two * mlp).astype(half)
        upstream = cot_ref[0].astype(full)
        d_gate_two = jnp.sum(upstream * mlp, axis=0, keepdims=True)
        e_mlp = upstream * gate_two
        sum_mlp = jnp.sum(e_mlp, axis=0, keepdims=True)
        d_mlp = e_mlp.astype(half)
        d_h_two = None
        for j in range(chunks):
            cols = slice(j * features, (j + 1) * features)
            acc_down[:, cols] += dot_tn(d_mlp, hidden_ref[:, cols])
            e_pre = dot_nt(d_mlp, down_ref[cols, :]) * slope_ref[:, cols]
            vec_ref[4:5, cols] += jnp.sum(e_pre, axis=0, keepdims=True)
            d_pre = e_pre.astype(half)
            acc_up[j] += dot_tn(h_two, d_pre)
            term = dot_nt(d_pre, up_ref[j])
            d_h_two = term if d_h_two is None else d_h_two + term
        d_scale_two = jnp.sum(d_h_two * normed_two, axis=0, keepdims=True)
        d_shift_two = jnp.sum(d_h_two, axis=0, keepdims=True)
        d_mid = upstream + norm_back(normed_two, inv_two, d_h_two * (1.0 + scale_two))
        d_gate_one = jnp.sum(d_mid * proj_ref[0], axis=0, keepdims=True)
        sum_proj = jnp.sum(d_mid, axis=0, keepdims=True) * gate_one
        dmid_ref[0] = d_mid
        vec_ref[5:6, :features] += sum_proj
        vec_ref[5:6, features : 2 * features] += sum_mlp
        vec_ref[pl.ds(slot, 1), :] = jnp.concatenate(
            [d_gate_one, d_shift_two, d_scale_two, d_gate_two], axis=1
        )

    @pl.when(slot == pl.num_programs(0) - 1)
    def _():
        lane = lax.broadcasted_iota(jnp.int32, (1, wide), 1)
        codes = jnp.zeros((1, wide), full)
        for row in range(8):
            label = info_ref[4 + row]
            high = (label >> 5).astype(full)
            low = (label & 31).astype(full)
            codes = jnp.where(lane == row, high, codes)
            codes = jnp.where(lane == 8 + row, low, codes)
        vec_ref[6:7, :] = codes
        note_ref[...] = vec_ref[...].astype(half)
        if keep_ref.ndim == 2:
            for j in range(chunks):
                keep_ref[:, j * features : (j + 1) * features] = acc_up[j].astype(half)
            send_ref[...] = acc_down[...].T.astype(half)
            return
        down_t[...] = acc_down[...].T
        chips, groups, _, rows, _ = keep_ref.shape
        for flip, target in enumerate((keep_ref, send_ref)):
            core = info_ref[1] ^ flip
            for hop in range(chips):
                for step in range(groups):
                    chip = info_ref[2] ^ hop
                    group = info_ref[3] ^ step
                    top = pl.multiple_of((group * 2 + core) * rows, rows)
                    target[hop, step, 0] = acc_up[chip, pl.ds(top, rows), :].astype(half)
                    top = pl.multiple_of(((group * chips + chip) * 2 + core) * rows, rows)
                    target[hop, step, 1] = down_t[pl.ds(top, rows), :].astype(half)


def attn_backward(
    info_ref, tok_ref, mod_ref, qkv_ref, prob_ref, attn_ref, dmid_ref, two_ref, *rest
):
    *parts, grad_ref, keep_ref, send_ref, note_ref, vec_ref, d_qkv_ref, acc_ref, weight_ref = rest
    features = tok_ref.shape[2]
    slot = pl.program_id(0)

    @pl.when(slot == 0)
    def _():
        load_first(info_ref, weight_ref, parts)
        acc_ref[...] = jnp.zeros_like(acc_ref)
        vec_ref[...] = jnp.zeros_like(vec_ref)

    @pl.when(slot >= info_ref[0])
    def _():
        grad_ref[...] = jnp.zeros_like(grad_ref)

    @pl.when(slot < info_ref[0])
    def _():
        mods = mod_ref[0]
        shift_one = mods[:, :features]
        scale_one = mods[:, features : 2 * features]
        gate_one = mods[:, 2 * features : 3 * features]
        normed_one, inv_one = layer_norm(tok_ref[0].astype(full))
        h_one = (normed_one * (1.0 + scale_one) + shift_one).astype(half)
        d_mid = dmid_ref[0]
        d_proj = (d_mid * gate_one).astype(half)
        acc_ref[:, 3 * features :] += dot_tn(attn_ref[0], d_proj)
        d_attn = dot_nt(d_proj, weight_ref[:, 3 * features :]).astype(half)
        masks = head_masks()
        width = 2 * HD
        for pair in range(HEADS // 2):
            low = pair * width
            queries = qkv_ref[0, :, low : low + width]
            keys_h = qkv_ref[0, :, features + low : features + low + width]
            values_h = qkv_ref[0, :, 2 * features + low : 2 * features + low + width]
            d_heads = d_attn[:, low : low + width]
            product = d_heads.astype(full) * attn_ref[0, :, low : low + width].astype(full)
            sums = [None, None, None]
            for side in range(2):
                mask = masks[side]
                probs = prob_ref[0, 2 * pair + side]
                d_side = d_heads * mask.astype(half)
                delta = jnp.sum(product * mask, axis=-1, keepdims=True)
                d_prob = dot_nt(d_side, values_h)
                d_scores = (probs.astype(full) * (d_prob - delta)).astype(half)
                scaled = (mask * HD ** (-0.5)).astype(half)
                terms = (
                    dot_nn(d_scores, keys_h * scaled),
                    dot_tn(d_scores, queries * scaled),
                    dot_tn(probs, d_side),
                )
                sums = [
                    term if total is None else total + term for total, term in zip(sums, terms)
                ]
            for part in range(3):
                d_qkv_ref[:, part * features + low : part * features + low + width] = sums[
                    part
                ].astype(half)
            vec_ref[4:5, low : low + width] += jnp.sum(sums[0], axis=0, keepdims=True)
            vec_ref[4:5, features + low : features + low + width] += jnp.sum(
                sums[2], axis=0, keepdims=True
            )
        acc_ref[:, : 3 * features] += dot_tn(h_one, d_qkv_ref[...])
        d_h_one = dot_nt(d_qkv_ref[...], weight_ref[:, : 3 * features])
        d_scale_one = jnp.sum(d_h_one * normed_one, axis=0, keepdims=True)
        d_shift_one = jnp.sum(d_h_one, axis=0, keepdims=True)
        grad_ref[0] = (d_mid + norm_back(normed_one, inv_one, d_h_one * (1.0 + scale_one))).astype(
            half
        )
        vec_ref[pl.ds(slot, 1), :] = jnp.concatenate([d_shift_one, d_scale_one], axis=1)

    @pl.when(slot == pl.num_programs(0) - 1)
    def _():
        note_ref[:, : 2 * features] = vec_ref[...].astype(half)
        note_ref[:, 2 * features :] = two_ref[...]
        if keep_ref.ndim == 2:
            keep_ref[...] = acc_ref[...].astype(half)
            send_ref[...] = jnp.zeros_like(send_ref)
            return
        pieces, rows, cols = keep_ref.shape
        chips = acc_ref.shape[1] // cols
        groups = pieces // chips
        for flip, target in enumerate((keep_ref, send_ref)):
            core = info_ref[1] ^ flip
            for chip in range(chips):
                for group in range(groups):
                    top = pl.multiple_of((group * 2 + core) * rows, rows)
                    target[chip * groups + group] = acc_ref[
                        pl.ds(top, rows), chip * cols : (chip + 1) * cols
                    ].astype(half)


def per_slot(*extent):
    return pl.BlockSpec((1,) + extent, lambda slot, info: (slot,) + (0,) * len(extent))


def whole(*extent):
    return pl.BlockSpec(extent, lambda slot, info: (0,) * len(extent))


def run_kernel(kernel, steps, work, ins, outs, scratch, info, operands):
    return pl.pallas_call(
        kernel,
        grid_spec=pltpu.PrefetchScalarGridSpec(
            num_scalar_prefetch=1,
            grid=(steps,),
            in_specs=ins,
            out_specs=[spec for spec, _ in outs],
            scratch_shapes=scratch,
        ),
        out_shape=[shape for _, shape in outs],
        cost_estimate=pl.CostEstimate(
            flops=int(work), bytes_accessed=int(work) // 300, transcendentals=int(work) // 1000
        ),
    )(info, *operands)


def adamw_update(weight, gradient, mean, square):
    mean_new = beta_one * mean + (1.0 - beta_one) * gradient
    square_new = beta_two * square + (1.0 - beta_two) * gradient * gradient
    mean_hat = mean_new / (1.0 - beta_one**STEP)
    square_hat = square_new / (1.0 - beta_two**STEP)
    weight_new = weight - learn_rate * (
        mean_hat / (jnp.sqrt(square_hat) + adam_eps) + weight_decay * weight
    )
    return (weight_new, mean_new, square_new)


def swap(values, axis, step):
    count = lax.axis_size(axis)
    return lax.ppermute(values, axis, [(i, i ^ step) for i in range(count)])


def exchange(pieces, axes):
    return lax.all_to_all(pieces, axes, 0, 0, tiled=True)


def spread(values, count, axes):
    return exchange(jnp.broadcast_to(values[None], (count,) + values.shape), axes)


def neighbours(values, axis):
    return [values] + [swap(values, axis, k) for k in range(1, lax.axis_size(axis))]


def after(values, first):
    return lax.optimization_barrier((values, first))[0]


def order(pieces, index):
    buffer = jnp.zeros((len(pieces),) + pieces[0].shape, pieces[0].dtype)
    for step, piece in enumerate(pieces):
        buffer = lax.dynamic_update_index_in_dim(buffer, piece, index ^ step, 0)
    return buffer


def choose(values, index):
    return lax.dynamic_index_in_dim(values, index, 0, keepdims=False)


def add_up(pieces):
    return jnp.sum(pieces.astype(full), axis=0)


def body(
    reps,
    groups,
    tokens,
    cotangent,
    cond_table,
    labels,
    counts,
    mod_weight,
    qkv_weight,
    out_weight,
    up_weight,
    down_weight,
    biases,
    mod_mean,
    qkv_mean,
    out_mean,
    up_mean,
    down_mean,
    bias_mean,
    mod_square,
    qkv_square,
    out_square,
    up_square,
    down_square,
    bias_square,
):
    cores = 2
    chips = reps // cores
    devices = reps * groups
    core = lax.axis_index("core")
    chip = lax.axis_index("chip")
    group = lax.axis_index("fsdp")
    capacity, length, features = tokens.shape
    classes_all = cond_table.shape[0]
    wide = up_weight.shape[1]
    shard = features // groups
    rows = shard // cores
    cols = wide // chips
    down_rows = wide // (devices)
    aligned = rows % 16 == 0 and cols % 128 == 0 and (rows, cols) == (down_rows, features)

    live = lax.iota(jnp.int32, capacity) < counts[0]
    own_labels = jnp.where(live, labels, -1)
    head = jnp.concatenate([own_labels.astype(full), lax.reduce_precision(biases, 8, 7)])
    heads = spread(head[None], groups, "fsdp")[:, 0]
    group_labels = heads[:, :capacity].astype(jnp.int32)
    bias_full = heads[:, capacity:].reshape(-1)

    first_own = jnp.concatenate(
        [
            lax.dynamic_slice_in_dim(qkv_weight, core * rows, rows, 0),
            lax.dynamic_slice_in_dim(out_weight, core * rows, rows, 0),
        ],
        axis=1,
    ).astype(half)
    first_own = neighbours(first_own, "fsdp")
    first_other = [swap(part, "core", 1) for part in first_own]

    second_up = lax.dynamic_slice(up_weight, (core * rows, chip * cols), (rows, cols))
    second_down = lax.dynamic_slice_in_dim(
        down_weight, (chip * cores + core) * down_rows, down_rows, 0
    )
    if aligned:
        second_own = jnp.stack([second_up, second_down])
    else:
        second_own = jnp.concatenate([second_up.reshape(-1), second_down.reshape(-1)])
    second_own = jnp.stack(neighbours(second_own.astype(half), "fsdp"))
    second_own = neighbours(second_own, "chip")

    mod_half = mod_weight.astype(half)
    column = group * shard
    group_cond = cond_table[jnp.maximum(group_labels.reshape(-1), 0)]
    group_cond = lax.dynamic_slice_in_dim(group_cond, column, shard, 1).astype(full)
    partial = jnp.dot(
        jax.nn.silu(group_cond).astype(half), mod_half, preferred_element_type=full
    ).reshape(groups, capacity, 6 * features)
    modulation = add_up(exchange(partial, "fsdp")) + bias_full[: 6 * features]
    modulation = modulation[:, None, :]

    if aligned:
        first_parts = first_own + first_other
    else:
        first_all = order([order(first_own, group), order(first_other, group)], core)
        first_parts = [first_all.transpose(1, 0, 2, 3).reshape(features, wide)]

    info = jnp.concatenate(
        [
            jnp.stack([counts[0], core, chip, group]).astype(jnp.int32),
            own_labels,
            jnp.full((8 - capacity,), -1, jnp.int32),
        ]
    )
    nothing = jnp.zeros((features,), full)
    b0 = 6 * features
    first_bias = jnp.concatenate(
        [
            bias_full[b0 : b0 + features],
            nothing,
            bias_full[b0 + features : b0 + 3 * features],
        ]
    )[None]
    second_bias = bias_full[b0 + 3 * features :][None]
    slot_tok = per_slot(length, features)
    slot_mod = per_slot(1, 6 * features)
    first_specs = [whole(*part.shape) for part in first_parts]
    work = 2 * capacity * length * features * wide * 4

    def shaped(dtype, *extent):
        return jax.ShapeDtypeStruct(extent, dtype)

    qkv_rows, probs, attn_out, proj = run_kernel(
        attn_forward,
        capacity,
        2 * work,
        [slot_tok, slot_mod, whole(1, wide), *first_specs],
        [
            (per_slot(length, 3 * features), shaped(half, capacity, length, 3 * features)),
            (per_slot(HEADS, length, length), shaped(half, capacity, HEADS, length, length)),
            (slot_tok, shaped(half, capacity, length, features)),
            (slot_tok, shaped(full, capacity, length, features)),
        ],
        [pltpu.VMEM((features, wide), half)],
        info,
        (tokens, modulation, first_bias, *first_parts),
    )

    second_own, proj = lax.optimization_barrier((second_own, proj))
    second_other = [swap(part, "core", 1) for part in second_own]
    if aligned:
        second_parts = second_own + second_other
    else:
        second_all = order(
            [
                order([order(list(part), group) for part in side], chip)
                for side in (second_own, second_other)
            ],
            core,
        )
        border = rows * cols
        second_parts = [
            second_all[..., :border]
            .reshape(cores, chips, groups, rows, cols)
            .transpose(2, 0, 3, 1, 4)
            .reshape(features, wide),
            second_all[..., border:]
            .reshape(cores, chips, groups, down_rows, features)
            .transpose(2, 1, 0, 3, 4)
            .reshape(wide, features),
        ]
    second_specs = [whole(*part.shape) for part in second_parts]

    if aligned:
        first_packs = [(chips * groups, rows, cols)] * 2
        second_packs = [(chips, groups, 2, rows, cols)] * 2
    else:
        first_packs = [(features, wide), (8, 128)]
        second_packs = [(features, wide), (wide, features)]
    block_out, d_mid, second_keep, second_send, note_two = run_kernel(
        functools.partial(mlp_both, len(second_parts)),
        capacity,
        4 * work,
        [
            slot_tok,
            slot_tok,
            slot_mod,
            slot_tok,
            whole(1, wide + features),
            *second_specs,
        ],
        [
            (slot_tok, shaped(half, capacity, length, features)),
            (slot_tok, shaped(full, capacity, length, features)),
            *[(whole(*pack), shaped(half, *pack)) for pack in second_packs],
            (whole(8, wide), shaped(half, 8, wide)),
        ],
        [
            pltpu.VMEM((8, wide), full),
            pltpu.VMEM((length, wide), half),
            pltpu.VMEM((length, wide), full),
            pltpu.VMEM((wide // features, features, features), full),
            pltpu.VMEM((features, wide), full),
            pltpu.VMEM((wide, features), full),
            pltpu.VMEM((wide // features, features, features), half),
            pltpu.VMEM((wide, features), half),
        ],
        info,
        (tokens, cotangent, modulation, proj, second_bias, *second_parts),
    )
    if not aligned:
        up_part = (
            second_keep.reshape(groups, cores, rows, chips, cols)
            .transpose(1, 3, 0, 2, 4)
            .reshape(cores, chips, groups, -1)
        )
        down_part = (
            second_send.reshape(groups, chips, cores, down_rows, features)
            .transpose(2, 1, 0, 3, 4)
            .reshape(cores, chips, groups, -1)
        )
        packed = jnp.concatenate([up_part, down_part], axis=-1)
        packed = packed[:, lax.iota(jnp.int32, chips) ^ chip]
        packed = packed[:, :, lax.iota(jnp.int32, groups) ^ group]
        second_keep, second_send = choose(packed, core), choose(packed, 1 - core)
    second_back = swap(second_send, "core", 1)
    by_chip = [
        (second_keep[k].astype(full) + second_back[k].astype(full)).astype(half)
        for k in range(chips)
    ]
    by_chip = [by_chip[0]] + [swap(by_chip[k], "chip", k) for k in range(1, chips)]
    token_grad, first_keep, first_send, note = run_kernel(
        attn_backward,
        capacity,
        3 * work,
        [
            slot_tok,
            slot_mod,
            per_slot(length, 3 * features),
            per_slot(HEADS, length, length),
            slot_tok,
            slot_tok,
            whole(8, wide),
            *first_specs,
        ],
        [
            (slot_tok, shaped(half, capacity, length, features)),
            *[(whole(*pack), shaped(half, *pack)) for pack in first_packs],
            (whole(8, 6 * features), shaped(half, 8, 6 * features)),
        ],
        [
            pltpu.VMEM((8, 2 * features), full),
            pltpu.VMEM((length, 3 * features), half),
            pltpu.VMEM((features, wide), full),
            pltpu.VMEM((features, wide), half),
        ],
        info,
        (tokens, modulation, qkv_rows, probs, attn_out, d_mid, note_two, *first_parts),
    )
    if not aligned:
        packed = (
            first_keep.reshape(groups, cores, rows, chips, cols)
            .transpose(1, 3, 0, 2, 4)
            .reshape(cores, chips * groups, rows, cols)
        )
        first_keep, first_send = choose(packed, core), choose(packed, 1 - core)
    first_back = swap(first_send, "core", 1)
    first_sum = (first_keep.astype(full) + first_back.astype(full)).astype(half)
    pieces = exchange(first_sum, ("chip", "fsdp"))
    by_chip = after(by_chip, first_sum)

    by_group = []
    for k in range(groups):
        total = by_chip[0][k].astype(full)
        for part in by_chip[1:]:
            total = total + part[k].astype(full)
        by_group.append(total.astype(half))
    second_sum = by_group[0].astype(full)
    for k in range(1, groups):
        second_sum = second_sum + swap(by_group[k], "fsdp", k).astype(full)
    second_sum = second_sum.astype(half)

    note = jnp.stack(neighbours(note, "fsdp"))
    note = jnp.stack(neighbours(note, "chip"))

    first_sum = add_up(pieces).astype(half)
    if aligned:
        third = jnp.concatenate([second_sum, first_sum[None]])
    else:
        third = jnp.concatenate([second_sum, first_sum.reshape(-1)])
    note = after(jnp.stack(neighbours(note, "core")), third)
    third = spread(third, reps, ("chip", "core")).reshape(chips, cores, *third.shape)
    if aligned:
        up_all, down_all, first_all = third[:, :, 0], third[:, :, 1], third[:, :, 2]
    else:
        border = rows * cols
        up_all = third[..., :border].reshape(chips, cores, rows, cols)
        down_all = third[..., border : border + down_rows * features]
        first_all = third[..., border + down_rows * features :]
        first_all = first_all.reshape(chips, cores, rows, cols)
    up_grad = up_all.transpose(1, 2, 0, 3).reshape(shard, wide).astype(full)
    down_grad = down_all.reshape(down_weight.shape).astype(full)
    first_grad = first_all.transpose(1, 2, 0, 3).reshape(shard, wide).astype(full)
    qkv_grad = first_grad[:, : 3 * features]
    out_grad = first_grad[:, 3 * features :]

    count = devices * 8
    line = lax.iota(jnp.int32, count) % 8
    note = note.reshape(devices, 8, 6 * features)
    label_notes = note[:, 6, 2 * features : 2 * features + 16].astype(jnp.int32)
    all_labels = (32 * label_notes[:, :8] + label_notes[:, 8:]).reshape(-1)
    d_mod = note.reshape(count, 6 * features)
    all_cond = cond_table[jnp.maximum(all_labels, 0)]
    all_cond = lax.dynamic_slice_in_dim(all_cond, column, shard, 1).astype(full)
    all_live = (all_labels >= 0)[:, None]
    sigmoid_c = jax.nn.sigmoid(all_cond)
    all_active = jnp.where(all_live, all_cond * sigmoid_c, 0.0).astype(half)
    slope_c = jnp.where(all_live, sigmoid_c * (1.0 + all_cond * (1.0 - sigmoid_c)), 0.0)
    mod_grad = dot_tn(all_active, d_mod)
    d_act = dot_nt(d_mod, mod_half)
    picks = jnp.stack([line < capacity, line == 4, line == 5]).astype(half)
    sums = dot_nn(picks, d_mod)
    d_cond = neighbours((d_act * slope_c).astype(half), "fsdp")
    class_share = classes_all // groups
    class_ids = lax.iota(jnp.int32, class_share) + group * class_share
    by_place = all_labels.reshape(reps, groups, 8)
    tables = []
    for k in range(groups):
        seen = jnp.concatenate([by_place[:, g ^ k : (g ^ k) + 1] for g in range(groups)], axis=1)
        chosen = (class_ids[:, None] == seen.reshape(1, -1)).astype(half)
        tables.append(dot_nn(chosen, d_cond[k]))
    table_grad = order(tables, group).transpose(1, 0, 2).reshape(class_share, features)
    two = 2 * features
    bias_all = jnp.concatenate(
        [
            sums[0],
            sums[1, :two],
            sums[2, two : two + features],
            sums[1, two:],
            sums[2, two + features : 2 * two],
        ]
    )
    bias_share = biases.shape[0]
    bias_grad = lax.dynamic_slice_in_dim(bias_all, group * bias_share, bias_share, 0)

    mod_next, mean_mod, square_mod = adamw_update(mod_weight, mod_grad, mod_mean, mod_square)
    qkv_next, mean_qkv, square_qkv = adamw_update(qkv_weight, qkv_grad, qkv_mean, qkv_square)
    out_next, mean_out, square_out = adamw_update(out_weight, out_grad, out_mean, out_square)
    up_next, mean_up, square_up = adamw_update(up_weight, up_grad, up_mean, up_square)
    down_next, mean_down, square_down = adamw_update(down_weight, down_grad, down_mean, down_square)
    bias_next, mean_bias, square_bias = adamw_update(biases, bias_grad, bias_mean, bias_square)
    return (
        block_out,
        token_grad,
        table_grad,
        mod_grad,
        qkv_grad,
        out_grad,
        up_grad,
        down_grad,
        bias_grad,
        mod_next,
        qkv_next,
        out_next,
        up_next,
        down_next,
        bias_next,
        mean_mod,
        mean_qkv,
        mean_out,
        mean_up,
        mean_down,
        mean_bias,
        square_mod,
        square_qkv,
        square_out,
        square_up,
        square_down,
        square_bias,
    )


def solution(mesh):
    placed = (
        P(("chip", "core", "fsdp"), None, None),
        P(("chip", "core", "fsdp"), None, None),
        P(),
        P(("chip", "core", "fsdp")),
        P(("chip", "core", "fsdp")),
        P("fsdp", None),
        P("fsdp", None),
        P("fsdp", None),
        P("fsdp", None),
        P("fsdp", None),
        P("fsdp"),
        P("fsdp", None),
        P("fsdp", None),
        P("fsdp", None),
        P("fsdp", None),
        P("fsdp", None),
        P("fsdp"),
        P("fsdp", None),
        P("fsdp", None),
        P("fsdp", None),
        P("fsdp", None),
        P("fsdp", None),
        P("fsdp"),
    )
    reps, groups = mesh.shape["rep"], mesh.shape["fsdp"]
    fine = Mesh(mesh.devices.reshape(reps // 2, 2, groups), ("chip", "core", "fsdp"))
    return jax.shard_map(
        functools.partial(body, reps, groups),
        mesh=fine,
        in_specs=placed,
        out_specs=(
            P(("chip", "core", "fsdp"), None, None),
            P(("chip", "core", "fsdp"), None, None),
            P("fsdp", None),
            P("fsdp", None),
            P("fsdp", None),
            P("fsdp", None),
            P("fsdp", None),
            P("fsdp", None),
            P("fsdp"),
            P("fsdp", None),
            P("fsdp", None),
            P("fsdp", None),
            P("fsdp", None),
            P("fsdp", None),
            P("fsdp"),
            P("fsdp", None),
            P("fsdp", None),
            P("fsdp", None),
            P("fsdp", None),
            P("fsdp", None),
            P("fsdp"),
            P("fsdp", None),
            P("fsdp", None),
            P("fsdp", None),
            P("fsdp", None),
            P("fsdp", None),
            P("fsdp"),
        ),
        check_vma=False,
    )
```

```python
import functools

import jax
import jax.numpy as jnp
from jax import lax
from jax.experimental import pallas as pl
from jax.experimental.pallas import tpu as pltpu
from jax.sharding import Mesh
from jax.sharding import PartitionSpec as P

HEADS = 6
HD = 64
STEP = 5


norm_eps = 1e-06
beta_one = 0.9
beta_two = 0.999
adam_eps = 1e-08
learn_rate = 0.01
weight_decay = 0.1
gelu_coef = 0.7978845608
cubic_coef = 0.044715
half = jnp.bfloat16
full = jnp.float32


def dot_nn(left, right):
    return lax.dot_general(left, right, (((1,), (0,)), ((), ())), preferred_element_type=full)


def dot_nt(left, right):
    return lax.dot_general(left, right, (((1,), (1,)), ((), ())), preferred_element_type=full)


def dot_tn(left, right):
    return lax.dot_general(left, right, (((0,), (0,)), ((), ())), preferred_element_type=full)


def layer_norm(values):
    centre = values - jnp.mean(values, axis=-1, keepdims=True)
    inverse = lax.rsqrt(jnp.mean(centre * centre, axis=-1, keepdims=True) + norm_eps)
    return (centre * inverse, inverse)


def norm_back(normed, inverse, upstream):
    return inverse * (
        upstream
        - jnp.mean(upstream, axis=-1, keepdims=True)
        - normed * jnp.mean(upstream * normed, axis=-1, keepdims=True)
    )


def head_masks():
    lane = lax.broadcasted_iota(jnp.int32, (1, 2 * HD), 1)
    low = jnp.where(lane < HD, 1.0, 0.0).astype(full)
    return (low, 1.0 - low)


def load_first(info_ref, weight_ref, parts):
    if len(parts) == 1:
        weight_ref[...] = parts[0][...]
        return
    groups = len(parts) // 2
    rows = parts[0].shape[0]
    for flip in range(2):
        for step in range(groups):
            core = info_ref[1] ^ flip
            group = info_ref[3] ^ step
            top = pl.multiple_of((group * 2 + core) * rows, rows)
            weight_ref[pl.ds(top, rows), :] = parts[flip * groups + step][...]


def load_second(info_ref, up_ref, down_ref, parts):
    width = up_ref.shape[2]
    if parts[0].ndim == 2:
        for chunk in range(up_ref.shape[0]):
            up_ref[chunk] = parts[0][:, chunk * width : (chunk + 1) * width]
        down_ref[...] = parts[1][...]
        return
    chips = len(parts) // 2
    groups, _, rows, _ = parts[0].shape
    for flip in range(2):
        for hop in range(chips):
            for step in range(groups):
                core = info_ref[1] ^ flip
                chip = info_ref[2] ^ hop
                group = info_ref[3] ^ step
                source = parts[flip * chips + hop]
                top = pl.multiple_of((group * 2 + core) * rows, rows)
                up_ref[chip, pl.ds(top, rows), :] = source[step, 0]
                top = pl.multiple_of(((group * chips + chip) * 2 + core) * rows, rows)
                down_ref[pl.ds(top, rows), :] = source[step, 1]


def attn_forward(info_ref, tok_ref, mod_ref, bias_ref, *rest):
    *parts, qkv_ref, prob_ref, attn_ref, proj_ref, weight_ref = rest
    features = tok_ref.shape[2]

    @pl.when(pl.program_id(0) == 0)
    def _():
        load_first(info_ref, weight_ref, parts)

    @pl.when(pl.program_id(0) < info_ref[0])
    def _():
        mods = mod_ref[0]
        shift_one = mods[:, :features]
        scale_one = mods[:, features : 2 * features]
        inputs = tok_ref[0].astype(full)
        normed_one, _ = layer_norm(inputs)
        h_one = (normed_one * (1.0 + scale_one) + shift_one).astype(half)
        masks = head_masks()
        qkv_ref[0] = (
            dot_nn(h_one, weight_ref[:, : 3 * features]) + bias_ref[:, : 3 * features]
        ).astype(half)
        width = 2 * HD
        for pair in range(HEADS // 2):
            low = pair * width
            queries = qkv_ref[0, :, low : low + width]
            keys_h = qkv_ref[0, :, features + low : features + low + width]
            values_h = qkv_ref[0, :, 2 * features + low : 2 * features + low + width]
            total = None
            for side in range(2):
                scaled = queries * (masks[side] * HD ** (-0.5)).astype(half)
                exponent = jnp.exp(dot_nt(scaled, keys_h))
                row_total = jnp.sum(exponent, axis=-1, keepdims=True)
                probs = (exponent * (1.0 / row_total)).astype(half)
                prob_ref[0, 2 * pair + side] = probs
                term = dot_nn(probs, values_h * masks[side].astype(half))
                total = term if total is None else total + term
            attn_ref[0, :, low : low + width] = total.astype(half)
        proj_ref[0] = (
            dot_nn(attn_ref[0], weight_ref[:, 3 * features :]) + bias_ref[:, 3 * features :]
        )


def mlp_both(count_parts, info_ref, tok_ref, cot_ref, mod_ref, proj_ref, bias_ref, *rest):
    features = tok_ref.shape[2]
    parts = rest[:count_parts]
    out_ref, dmid_ref, keep_ref, send_ref, note_ref, *rest = rest[count_parts:]
    vec_ref, hidden_ref, slope_ref, acc_up, acc_down, down_t, up_ref, down_ref = rest
    wide = hidden_ref.shape[1]
    slot = pl.program_id(0)
    chunks = wide // features

    @pl.when(slot == 0)
    def _():
        load_second(info_ref, up_ref, down_ref, parts)
        acc_up[...] = jnp.zeros_like(acc_up)
        acc_down[...] = jnp.zeros_like(acc_down)
        vec_ref[...] = jnp.zeros_like(vec_ref)

    @pl.when(slot >= info_ref[0])
    def _():
        out_ref[...] = jnp.zeros_like(out_ref)

    @pl.when(slot < info_ref[0])
    def _():
        mods = mod_ref[0]
        gate_one = mods[:, 2 * features : 3 * features]
        shift_two = mods[:, 3 * features : 4 * features]
        scale_two = mods[:, 4 * features : 5 * features]
        gate_two = mods[:, 5 * features :]
        residual = tok_ref[0].astype(full) + gate_one * proj_ref[0]
        normed_two, inv_two = layer_norm(residual)
        h_two = (normed_two * (1.0 + scale_two) + shift_two).astype(half)
        mlp = None
        for j in range(chunks):
            cols = slice(j * features, (j + 1) * features)
            pre = dot_nn(h_two, up_ref[j]) + bias_ref[:, cols]
            square = pre * pre
            tanh_value = jnp.tanh(pre * (gelu_coef + gelu_coef * cubic_coef * square))
            gate = 0.5 + 0.5 * tanh_value
            hidden = pre * gate
            slope_ref[:, cols] = gate + hidden * (1.0 - gate) * (
                2.0 * gelu_coef + 6.0 * gelu_coef * cubic_coef * square
            )
            hidden_ref[:, cols] = hidden.astype(half)
            term = dot_nn(hidden_ref[:, cols], down_ref[cols, :])
            mlp = term if mlp is None else mlp + term
        mlp = mlp + bias_ref[:, wide:]
        out_ref[0] = (residual + gate_two * mlp).astype(half)
        upstream = cot_ref[0].astype(full)
        d_gate_two = jnp.sum(upstream * mlp, axis=0, keepdims=True)
        e_mlp = upstream * gate_two
        sum_mlp = jnp.sum(e_mlp, axis=0, keepdims=True)
        d_mlp = e_mlp.astype(half)
        d_h_two = None
        for j in range(chunks):
            cols = slice(j * features, (j + 1) * features)
            acc_down[:, cols] += dot_tn(d_mlp, hidden_ref[:, cols])
            e_pre = dot_nt(d_mlp, down_ref[cols, :]) * slope_ref[:, cols]
            vec_ref[4:5, cols] += jnp.sum(e_pre, axis=0, keepdims=True)
            d_pre = e_pre.astype(half)
            acc_up[j] += dot_tn(h_two, d_pre)
            term = dot_nt(d_pre, up_ref[j])
            d_h_two = term if d_h_two is None else d_h_two + term
        d_scale_two = jnp.sum(d_h_two * normed_two, axis=0, keepdims=True)
        d_shift_two = jnp.sum(d_h_two, axis=0, keepdims=True)
        d_mid = upstream + norm_back(normed_two, inv_two, d_h_two * (1.0 + scale_two))
        d_gate_one = jnp.sum(d_mid * proj_ref[0], axis=0, keepdims=True)
        sum_proj = jnp.sum(d_mid, axis=0, keepdims=True) * gate_one
        dmid_ref[0] = d_mid
        vec_ref[5:6, :features] += sum_proj
        vec_ref[5:6, features : 2 * features] += sum_mlp
        vec_ref[pl.ds(slot, 1), :] = jnp.concatenate(
            [d_gate_one, d_shift_two, d_scale_two, d_gate_two], axis=1
        )

    @pl.when(slot == pl.num_programs(0) - 1)
    def _():
        lane = lax.broadcasted_iota(jnp.int32, (1, wide), 1)
        codes = jnp.zeros((1, wide), full)
        for row in range(8):
            label = info_ref[4 + row]
            high = (label >> 5).astype(full)
            low = (label & 31).astype(full)
            codes = jnp.where(lane == row, high, codes)
            codes = jnp.where(lane == 8 + row, low, codes)
        vec_ref[6:7, :] = codes
        note_ref[...] = vec_ref[...].astype(half)
        if keep_ref.ndim == 2:
            for j in range(chunks):
                keep_ref[:, j * features : (j + 1) * features] = acc_up[j].astype(half)
            send_ref[...] = acc_down[...].T.astype(half)
            return
        down_t[...] = acc_down[...].T
        chips, groups, _, rows, _ = keep_ref.shape
        for flip, target in enumerate((keep_ref, send_ref)):
            core = info_ref[1] ^ flip
            for hop in range(chips):
                for step in range(groups):
                    chip = info_ref[2] ^ hop
                    group = info_ref[3] ^ step
                    top = pl.multiple_of((group * 2 + core) * rows, rows)
                    target[hop, step, 0] = acc_up[chip, pl.ds(top, rows), :].astype(half)
                    top = pl.multiple_of(((group * chips + chip) * 2 + core) * rows, rows)
                    target[hop, step, 1] = down_t[pl.ds(top, rows), :].astype(half)


def attn_backward(
    info_ref, tok_ref, mod_ref, qkv_ref, prob_ref, attn_ref, dmid_ref, two_ref, *rest
):
    *parts, grad_ref, keep_ref, send_ref, note_ref, vec_ref, d_qkv_ref, acc_ref, weight_ref = rest
    features = tok_ref.shape[2]
    slot = pl.program_id(0)

    @pl.when(slot == 0)
    def _():
        load_first(info_ref, weight_ref, parts)
        acc_ref[...] = jnp.zeros_like(acc_ref)
        vec_ref[...] = jnp.zeros_like(vec_ref)

    @pl.when(slot >= info_ref[0])
    def _():
        grad_ref[...] = jnp.zeros_like(grad_ref)

    @pl.when(slot < info_ref[0])
    def _():
        mods = mod_ref[0]
        shift_one = mods[:, :features]
        scale_one = mods[:, features : 2 * features]
        gate_one = mods[:, 2 * features : 3 * features]
        normed_one, inv_one = layer_norm(tok_ref[0].astype(full))
        h_one = (normed_one * (1.0 + scale_one) + shift_one).astype(half)
        d_mid = dmid_ref[0]
        d_proj = (d_mid * gate_one).astype(half)
        acc_ref[3] += dot_tn(attn_ref[0], d_proj)
        d_attn = dot_nt(d_proj, weight_ref[:, 3 * features :]).astype(half)
        masks = head_masks()
        width = 2 * HD
        for pair in range(HEADS // 2):
            low = pair * width
            queries = qkv_ref[0, :, low : low + width]
            keys_h = qkv_ref[0, :, features + low : features + low + width]
            values_h = qkv_ref[0, :, 2 * features + low : 2 * features + low + width]
            d_heads = d_attn[:, low : low + width]
            product = d_heads.astype(full) * attn_ref[0, :, low : low + width].astype(full)
            sums = [None, None, None]
            for side in range(2):
                mask = masks[side]
                probs = prob_ref[0, 2 * pair + side]
                d_side = d_heads * mask.astype(half)
                delta = jnp.sum(product * mask, axis=-1, keepdims=True)
                d_prob = dot_nt(d_side, values_h)
                d_scores = (probs.astype(full) * (d_prob - delta)).astype(half)
                scaled = (mask * HD ** (-0.5)).astype(half)
                terms = (
                    dot_nn(d_scores, keys_h * scaled),
                    dot_tn(d_scores, queries * scaled),
                    dot_tn(probs, d_side),
                )
                sums = [
                    term if total is None else total + term for total, term in zip(sums, terms)
                ]
            for part in range(3):
                d_qkv_ref[:, part * features + low : part * features + low + width] = sums[
                    part
                ].astype(half)
            vec_ref[4:5, low : low + width] += jnp.sum(sums[0], axis=0, keepdims=True)
            vec_ref[4:5, features + low : features + low + width] += jnp.sum(
                sums[2], axis=0, keepdims=True
            )
        for part in range(3):
            acc_ref[part] += dot_tn(h_one, d_qkv_ref[:, part * features : (part + 1) * features])
        d_h_one = dot_nt(d_qkv_ref[...], weight_ref[:, : 3 * features])
        d_scale_one = jnp.sum(d_h_one * normed_one, axis=0, keepdims=True)
        d_shift_one = jnp.sum(d_h_one, axis=0, keepdims=True)
        grad_ref[0] = (d_mid + norm_back(normed_one, inv_one, d_h_one * (1.0 + scale_one))).astype(
            half
        )
        vec_ref[pl.ds(slot, 1), :] = jnp.concatenate([d_shift_one, d_scale_one], axis=1)

    @pl.when(slot == pl.num_programs(0) - 1)
    def _():
        note_ref[:, : 2 * features] = vec_ref[...].astype(half)
        note_ref[:, 2 * features :] = two_ref[...]
        if keep_ref.ndim == 2:
            for part in range(4):
                keep_ref[:, part * features : (part + 1) * features] = acc_ref[part].astype(half)
            send_ref[...] = jnp.zeros_like(send_ref)
            return
        chips, groups, rows, _ = keep_ref.shape
        for flip, target in enumerate((keep_ref, send_ref)):
            core = info_ref[1] ^ flip
            for hop in range(chips):
                for step in range(groups):
                    chip = info_ref[2] ^ hop
                    group = info_ref[3] ^ step
                    top = pl.multiple_of((group * 2 + core) * rows, rows)
                    target[hop, step] = acc_ref[chip, pl.ds(top, rows), :].astype(half)


def per_slot(*extent):
    return pl.BlockSpec((1,) + extent, lambda slot, info: (slot,) + (0,) * len(extent))


def whole(*extent):
    return pl.BlockSpec(extent, lambda slot, info: (0,) * len(extent))


def run_kernel(kernel, steps, work, ins, outs, scratch, info, operands):
    return pl.pallas_call(
        kernel,
        grid_spec=pltpu.PrefetchScalarGridSpec(
            num_scalar_prefetch=1,
            grid=(steps,),
            in_specs=ins,
            out_specs=[spec for spec, _ in outs],
            scratch_shapes=scratch,
        ),
        out_shape=[shape for _, shape in outs],
        cost_estimate=pl.CostEstimate(
            flops=int(work), bytes_accessed=int(work) // 300, transcendentals=int(work) // 1000
        ),
    )(info, *operands)


def adamw_update(weight, gradient, mean, square):
    mean_new = beta_one * mean + (1.0 - beta_one) * gradient
    square_new = beta_two * square + (1.0 - beta_two) * gradient * gradient
    mean_hat = mean_new / (1.0 - beta_one**STEP)
    square_hat = square_new / (1.0 - beta_two**STEP)
    weight_new = weight - learn_rate * (
        mean_hat / (jnp.sqrt(square_hat) + adam_eps) + weight_decay * weight
    )
    return (weight_new, mean_new, square_new)


def swap(values, axis, step):
    count = lax.axis_size(axis)
    return lax.ppermute(values, axis, [(i, i ^ step) for i in range(count)])


def exchange(pieces, axes):
    return lax.all_to_all(pieces, axes, 0, 0, tiled=True)


def spread(values, count, axes):
    return exchange(jnp.broadcast_to(values[None], (count,) + values.shape), axes)


def neighbours(values, axis):
    return [values] + [swap(values, axis, k) for k in range(1, lax.axis_size(axis))]


def after(values, first):
    return lax.optimization_barrier((values, first))[0]


def order(pieces, index):
    buffer = jnp.zeros((len(pieces),) + pieces[0].shape, pieces[0].dtype)
    for step, piece in enumerate(pieces):
        buffer = lax.dynamic_update_index_in_dim(buffer, piece, index ^ step, 0)
    return buffer


def pair_sum(keep, back):
    return [
        (keep[k].astype(full) + back[k].astype(full)).astype(half) for k in range(keep.shape[0])
    ]


def group_sum(by_chip, groups):
    pieces = []
    for k in range(groups):
        total = by_chip[0][k].astype(full)
        for part in by_chip[1:]:
            total = total + part[k].astype(full)
        pieces.append(total.astype(half))
    total = pieces[0].astype(full)
    for k in range(1, groups):
        total = total + swap(pieces[k], "fsdp", k).astype(full)
    return total.astype(half)


def choose(values, index):
    return lax.dynamic_index_in_dim(values, index, 0, keepdims=False)


def add_up(pieces):
    return jnp.sum(pieces.astype(full), axis=0)


def body(
    reps,
    groups,
    tokens,
    cotangent,
    cond_table,
    labels,
    counts,
    mod_weight,
    qkv_weight,
    out_weight,
    up_weight,
    down_weight,
    biases,
    mod_mean,
    qkv_mean,
    out_mean,
    up_mean,
    down_mean,
    bias_mean,
    mod_square,
    qkv_square,
    out_square,
    up_square,
    down_square,
    bias_square,
):
    cores = 2
    chips = reps // cores
    devices = reps * groups
    core = lax.axis_index("core")
    chip = lax.axis_index("chip")
    group = lax.axis_index("fsdp")
    capacity, length, features = tokens.shape
    classes_all = cond_table.shape[0]
    wide = up_weight.shape[1]
    shard = features // groups
    rows = shard // cores
    cols = wide // chips
    down_rows = wide // (devices)
    aligned = rows % 16 == 0 and cols % 128 == 0 and (rows, cols) == (down_rows, features)

    def relative(packed):
        packed = packed[:, lax.iota(jnp.int32, chips) ^ chip]
        return packed[:, :, lax.iota(jnp.int32, groups) ^ group]

    live = lax.iota(jnp.int32, capacity) < counts[0]
    own_labels = jnp.where(live, labels, -1)
    head = jnp.concatenate([own_labels.astype(full), lax.reduce_precision(biases, 8, 7)])
    heads = spread(head[None], groups, "fsdp")[:, 0]
    group_labels = heads[:, :capacity].astype(jnp.int32)
    bias_full = heads[:, capacity:].reshape(-1)

    first_own = jnp.concatenate(
        [
            lax.dynamic_slice_in_dim(qkv_weight, core * rows, rows, 0),
            lax.dynamic_slice_in_dim(out_weight, core * rows, rows, 0),
        ],
        axis=1,
    ).astype(half)
    first_own = neighbours(first_own, "fsdp")
    first_other = [swap(part, "core", 1) for part in first_own]

    second_up = lax.dynamic_slice(up_weight, (core * rows, chip * cols), (rows, cols))
    second_down = lax.dynamic_slice_in_dim(
        down_weight, (chip * cores + core) * down_rows, down_rows, 0
    )
    if aligned:
        second_own = jnp.stack([second_up, second_down])
    else:
        second_own = jnp.concatenate([second_up.reshape(-1), second_down.reshape(-1)])
    second_own = jnp.stack(neighbours(second_own.astype(half), "fsdp"))
    second_own = neighbours(second_own, "chip")

    mod_half = mod_weight.astype(half)
    column = group * shard
    group_cond = cond_table[jnp.maximum(group_labels.reshape(-1), 0)]
    group_cond = lax.dynamic_slice_in_dim(group_cond, column, shard, 1).astype(full)
    partial = jnp.dot(
        jax.nn.silu(group_cond).astype(half), mod_half, preferred_element_type=full
    ).reshape(groups, capacity, 6 * features)
    modulation = add_up(exchange(partial, "fsdp")) + bias_full[: 6 * features]
    modulation = modulation[:, None, :]

    if aligned:
        first_parts = first_own + first_other
    else:
        first_all = order([order(first_own, group), order(first_other, group)], core)
        first_parts = [first_all.transpose(1, 0, 2, 3).reshape(features, wide)]

    info = jnp.concatenate(
        [
            jnp.stack([counts[0], core, chip, group]).astype(jnp.int32),
            own_labels,
            jnp.full((8 - capacity,), -1, jnp.int32),
        ]
    )
    nothing = jnp.zeros((features,), full)
    b0 = 6 * features
    first_bias = jnp.concatenate(
        [
            bias_full[b0 : b0 + features],
            nothing,
            bias_full[b0 + features : b0 + 3 * features],
        ]
    )[None]
    second_bias = bias_full[b0 + 3 * features :][None]
    slot_tok = per_slot(length, features)
    slot_mod = per_slot(1, 6 * features)
    first_specs = [whole(*part.shape) for part in first_parts]
    work = 2 * capacity * length * features * wide * 4

    def shaped(dtype, *extent):
        return jax.ShapeDtypeStruct(extent, dtype)

    qkv_rows, probs, attn_out, proj = run_kernel(
        attn_forward,
        capacity,
        2 * work,
        [slot_tok, slot_mod, whole(1, wide), *first_specs],
        [
            (per_slot(length, 3 * features), shaped(half, capacity, length, 3 * features)),
            (per_slot(HEADS, length, length), shaped(half, capacity, HEADS, length, length)),
            (slot_tok, shaped(half, capacity, length, features)),
            (slot_tok, shaped(full, capacity, length, features)),
        ],
        [pltpu.VMEM((features, wide), half)],
        info,
        (tokens, modulation, first_bias, *first_parts),
    )

    second_own, proj = lax.optimization_barrier((second_own, proj))
    second_other = [swap(part, "core", 1) for part in second_own]
    if aligned:
        second_parts = second_own + second_other
    else:
        second_all = order(
            [
                order([order(list(part), group) for part in side], chip)
                for side in (second_own, second_other)
            ],
            core,
        )
        border = rows * cols
        second_parts = [
            second_all[..., :border]
            .reshape(cores, chips, groups, rows, cols)
            .transpose(2, 0, 3, 1, 4)
            .reshape(features, wide),
            second_all[..., border:]
            .reshape(cores, chips, groups, down_rows, features)
            .transpose(2, 1, 0, 3, 4)
            .reshape(wide, features),
        ]
    second_specs = [whole(*part.shape) for part in second_parts]

    if aligned:
        first_packs = [(chips, groups, rows, cols)] * 2
        second_packs = [(chips, groups, 2, rows, cols)] * 2
    else:
        first_packs = [(features, wide), (8, 128)]
        second_packs = [(features, wide), (wide, features)]
    block_out, d_mid, second_keep, second_send, note_two = run_kernel(
        functools.partial(mlp_both, len(second_parts)),
        capacity,
        4 * work,
        [
            slot_tok,
            slot_tok,
            slot_mod,
            slot_tok,
            whole(1, wide + features),
            *second_specs,
        ],
        [
            (slot_tok, shaped(half, capacity, length, features)),
            (slot_tok, shaped(full, capacity, length, features)),
            *[(whole(*pack), shaped(half, *pack)) for pack in second_packs],
            (whole(8, wide), shaped(half, 8, wide)),
        ],
        [
            pltpu.VMEM((8, wide), full),
            pltpu.VMEM((length, wide), half),
            pltpu.VMEM((length, wide), full),
            pltpu.VMEM((wide // features, features, features), full),
            pltpu.VMEM((features, wide), full),
            pltpu.VMEM((wide, features), full),
            pltpu.VMEM((wide // features, features, features), half),
            pltpu.VMEM((wide, features), half),
        ],
        info,
        (tokens, cotangent, modulation, proj, second_bias, *second_parts),
    )
    if not aligned:
        up_part = (
            second_keep.reshape(groups, cores, rows, chips, cols)
            .transpose(1, 3, 0, 2, 4)
            .reshape(cores, chips, groups, -1)
        )
        down_part = (
            second_send.reshape(groups, chips, cores, down_rows, features)
            .transpose(2, 1, 0, 3, 4)
            .reshape(cores, chips, groups, -1)
        )
        packed = jnp.concatenate([up_part, down_part], axis=-1)
        packed = relative(packed)
        second_keep, second_send = choose(packed, core), choose(packed, 1 - core)
    second_back = swap(second_send, "core", 1)
    by_chip = pair_sum(second_keep, second_back)
    by_chip = [by_chip[0]] + [swap(by_chip[k], "chip", k) for k in range(1, chips)]
    token_grad, first_keep, first_send, note = run_kernel(
        attn_backward,
        capacity,
        3 * work,
        [
            slot_tok,
            slot_mod,
            per_slot(length, 3 * features),
            per_slot(HEADS, length, length),
            slot_tok,
            slot_tok,
            whole(8, wide),
            *first_specs,
        ],
        [
            (slot_tok, shaped(half, capacity, length, features)),
            *[(whole(*pack), shaped(half, *pack)) for pack in first_packs],
            (whole(8, 6 * features), shaped(half, 8, 6 * features)),
        ],
        [
            pltpu.VMEM((8, 2 * features), full),
            pltpu.VMEM((length, 3 * features), half),
            pltpu.VMEM((4, features, features), full),
            pltpu.VMEM((features, wide), half),
        ],
        info,
        (tokens, modulation, qkv_rows, probs, attn_out, d_mid, note_two, *first_parts),
    )
    if not aligned:
        packed = relative(
            first_keep.reshape(groups, cores, rows, chips, cols).transpose(1, 3, 0, 2, 4)
        )
        first_keep, first_send = choose(packed, core), choose(packed, 1 - core)
    first_back = swap(first_send, "core", 1)
    first_chip = pair_sum(first_keep, first_back)
    by_chip = after(by_chip, first_chip)
    first_chip = [first_chip[0]] + [swap(first_chip[k], "chip", k) for k in range(1, chips)]
    second_sum = group_sum(by_chip, groups)
    first_sum = group_sum(first_chip, groups)

    note = jnp.stack(after(neighbours(note, "fsdp"), first_chip[0]))
    note = neighbours(note, "chip")

    if aligned:
        third = jnp.concatenate([second_sum, first_sum[None]])
    else:
        third = jnp.concatenate([second_sum, first_sum.reshape(-1)])
    note = jnp.stack(after(note, third))
    note = jnp.stack(neighbours(note, "core"))
    third = spread(third, reps, ("chip", "core")).reshape(chips, cores, *third.shape)
    if aligned:
        up_all, down_all, first_all = third[:, :, 0], third[:, :, 1], third[:, :, 2]
    else:
        border = rows * cols
        up_all = third[..., :border].reshape(chips, cores, rows, cols)
        down_all = third[..., border : border + down_rows * features]
        first_all = third[..., border + down_rows * features :]
        first_all = first_all.reshape(chips, cores, rows, cols)
    up_grad = up_all.transpose(1, 2, 0, 3).reshape(shard, wide).astype(full)
    down_grad = down_all.reshape(down_weight.shape).astype(full)
    first_grad = first_all.transpose(1, 2, 0, 3).reshape(shard, wide).astype(full)
    qkv_grad = first_grad[:, : 3 * features]
    out_grad = first_grad[:, 3 * features :]

    count = devices * 8
    line = lax.iota(jnp.int32, count) % 8
    note = note.reshape(devices, 8, 6 * features)
    label_notes = note[:, 6, 2 * features : 2 * features + 16].astype(jnp.int32)
    all_labels = (32 * label_notes[:, :8] + label_notes[:, 8:]).reshape(-1)
    d_mod = note.reshape(count, 6 * features)
    all_cond = cond_table[jnp.maximum(all_labels, 0)]
    all_cond = lax.dynamic_slice_in_dim(all_cond, column, shard, 1).astype(full)
    all_live = (all_labels >= 0)[:, None]
    sigmoid_c = jax.nn.sigmoid(all_cond)
    all_active = jnp.where(all_live, all_cond * sigmoid_c, 0.0).astype(half)
    slope_c = jnp.where(all_live, sigmoid_c * (1.0 + all_cond * (1.0 - sigmoid_c)), 0.0)
    mod_grad = dot_tn(all_active, d_mod)
    d_act = dot_nt(d_mod, mod_half)
    picks = jnp.stack([line < capacity, line == 4, line == 5]).astype(half)
    sums = dot_nn(picks, d_mod)
    d_cond = neighbours((d_act * slope_c).astype(half), "fsdp")
    class_share = classes_all // groups
    class_ids = lax.iota(jnp.int32, class_share) + group * class_share
    by_place = all_labels.reshape(reps, groups, 8)
    tables = []
    for k in range(groups):
        seen = jnp.concatenate([by_place[:, g ^ k : (g ^ k) + 1] for g in range(groups)], axis=1)
        chosen = (class_ids[:, None] == seen.reshape(1, -1)).astype(half)
        tables.append(dot_nn(chosen, d_cond[k]))
    table_grad = order(tables, group).transpose(1, 0, 2).reshape(class_share, features)
    two = 2 * features
    bias_all = jnp.concatenate(
        [
            sums[0],
            sums[1, :two],
            sums[2, two : two + features],
            sums[1, two:],
            sums[2, two + features : 2 * two],
        ]
    )
    bias_share = biases.shape[0]
    bias_grad = lax.dynamic_slice_in_dim(bias_all, group * bias_share, bias_share, 0)

    mod_next, mean_mod, square_mod = adamw_update(mod_weight, mod_grad, mod_mean, mod_square)
    qkv_next, mean_qkv, square_qkv = adamw_update(qkv_weight, qkv_grad, qkv_mean, qkv_square)
    out_next, mean_out, square_out = adamw_update(out_weight, out_grad, out_mean, out_square)
    up_next, mean_up, square_up = adamw_update(up_weight, up_grad, up_mean, up_square)
    down_next, mean_down, square_down = adamw_update(down_weight, down_grad, down_mean, down_square)
    bias_next, mean_bias, square_bias = adamw_update(biases, bias_grad, bias_mean, bias_square)
    return (
        block_out,
        token_grad,
        table_grad,
        mod_grad,
        qkv_grad,
        out_grad,
        up_grad,
        down_grad,
        bias_grad,
        mod_next,
        qkv_next,
        out_next,
        up_next,
        down_next,
        bias_next,
        mean_mod,
        mean_qkv,
        mean_out,
        mean_up,
        mean_down,
        mean_bias,
        square_mod,
        square_qkv,
        square_out,
        square_up,
        square_down,
        square_bias,
    )


def solution(mesh):
    placed = (
        P(("chip", "core", "fsdp"), None, None),
        P(("chip", "core", "fsdp"), None, None),
        P(),
        P(("chip", "core", "fsdp")),
        P(("chip", "core", "fsdp")),
        P("fsdp", None),
        P("fsdp", None),
        P("fsdp", None),
        P("fsdp", None),
        P("fsdp", None),
        P("fsdp"),
        P("fsdp", None),
        P("fsdp", None),
        P("fsdp", None),
        P("fsdp", None),
        P("fsdp", None),
        P("fsdp"),
        P("fsdp", None),
        P("fsdp", None),
        P("fsdp", None),
        P("fsdp", None),
        P("fsdp", None),
        P("fsdp"),
    )
    reps, groups = mesh.shape["rep"], mesh.shape["fsdp"]
    fine = Mesh(mesh.devices.reshape(reps // 2, 2, groups), ("chip", "core", "fsdp"))
    return jax.shard_map(
        functools.partial(body, reps, groups),
        mesh=fine,
        in_specs=placed,
        out_specs=(
            P(("chip", "core", "fsdp"), None, None),
            P(("chip", "core", "fsdp"), None, None),
            P("fsdp", None),
            P("fsdp", None),
            P("fsdp", None),
            P("fsdp", None),
            P("fsdp", None),
            P("fsdp", None),
            P("fsdp"),
            P("fsdp", None),
            P("fsdp", None),
            P("fsdp", None),
            P("fsdp", None),
            P("fsdp", None),
            P("fsdp"),
            P("fsdp", None),
            P("fsdp", None),
            P("fsdp", None),
            P("fsdp", None),
            P("fsdp", None),
            P("fsdp"),
            P("fsdp", None),
            P("fsdp", None),
            P("fsdp", None),
            P("fsdp", None),
            P("fsdp", None),
            P("fsdp"),
        ),
        check_vma=False,
    )
```
